32 devices in a mesh: chan: 16 (over z, x, core), quad: 2 (over y).
Axes of the slice: x: 2, y: 2, z: 4, core: 2. Of those that a mesh axis runs over, the one named last changes fastest.
Arguments:
- voltages: float32 [2, 512, 1, 2, 8416], P('quad', 'chan'), may hold values from -6 to 6
- filter_taps: float32 [8, 32], replicated, may hold values from -0.375 to 0.375
- phases: int32 [32, 512, 1024], P('chan', None, 'quad'), may hold values from 0 to 255
Outputs:
- visibilities: float32 [32, 2, 1024, 1024], P('chan', None, 'quad')
- beam_power: float32 [32, 512, 256], P('chan', 'quad')
The draws below stay inside these ranges and needn't reach their ends.
All inputs are finite; a program needn't handle non-finite values.
Results may differ from the reference program's by a relative error of at most 0.0001.
Values sent between devices are 32-bit elements; how exact they have to be, the bound alone decides.
No kernel may reach another device: no remote copies, remote signals or barrier semaphores. Data moves between devices by JAX's collectives and lax.ppermute only.
A program may use at most 128 MiB of HBM per device.

```python
import math
import jax
import jax.numpy as jnp
from jax import lax

DISHES = 1024
FINE = 32
TAPS = 8
BEAMS = 512
PHASE_LEVELS = 256
MB = 2
SB = 128
COARSE = 1
CHANNELS = 32
SAMPLES = 8416
N_QUAD = 2


def with_ends(array, rng, low, high):
    dims = array.shape
    spot = [jax.random.randint(jax.random.fold_in(rng, axis), (), 0, dims[axis]) for axis in range(len(dims))]
    array = array.at[tuple(spot)].set(low)
    longest = dims.index(max(dims))
    spot[longest] = (spot[longest] + 1) % dims[longest]
    return array.at[tuple(spot)].set(high)


def steps_of(rng, shape, split, smallest, largest):
    gain = 1.0
    for position, blocks in split:
        steps = jax.random.uniform(jax.random.fold_in(jax.random.fold_in(rng, 6), position), (blocks,), jnp.float32, smallest / len(split), largest / len(split))
        gain = gain * jnp.repeat(jnp.exp(steps), shape[position] // blocks).reshape((-1,) + (1,) * (len(shape) - 1 - position))
    return gain


def centred(stream_key, dims, scale, limit, split=(), kind=jnp.bfloat16):
    drawn = scale * jax.random.normal(stream_key, dims, jnp.float32)
    if split:
        drawn = drawn * steps_of(stream_key, dims, split, -0.22, 0.18)
    return jnp.clip(drawn, -limit, limit).astype(kind)


def setup_inputs(seed: int = 0) -> dict:
    splits = jax.random.split(jax.random.key(seed), 4)
    voltages = centred(splits[0], (N_QUAD, DISHES // N_QUAD, COARSE, 2, SAMPLES), 1.0, 6.0, ((0, 2), (1, 16)), jnp.float32)
    filter_taps = centred(splits[1], (TAPS, FINE), (TAPS * FINE) ** -0.5, 0.375, (), jnp.float32)
    phases = with_ends(jax.random.randint(splits[2], (CHANNELS, BEAMS, DISHES), 0, PHASE_LEVELS), jax.random.fold_in(splits[2], 1), 0, PHASE_LEVELS - 1).astype(jnp.int32)
    return {"voltages": voltages, "filter_taps": filter_taps, "phases": phases}


highest = lax.Precision.HIGHEST


def dft_matrix():
    index_n = jnp.arange(FINE, dtype=jnp.int32)
    product = (index_n[:, None] * index_n[None, :]) % FINE
    angles = product.astype(jnp.float32) * (2.0 * math.pi / FINE)
    cosine = jnp.cos(angles)
    sine = jnp.sin(angles)
    return jnp.stack([jnp.stack([cosine, sine]), jnp.stack([-sine, cosine])])


def reference(voltages, filter_taps, phases):
    spectra_total = MB * SB
    frames = voltages.reshape(DISHES, COARSE, 2, spectra_total + TAPS - 1, FINE)
    filtered = jnp.zeros((DISHES, COARSE, 2, spectra_total, FINE), jnp.float32)
    for tap_index in range(TAPS):
        filtered = filtered + filter_taps[tap_index] * frames[:, :, :, tap_index:tap_index + spectra_total, :]
    spectra = jnp.einsum("dbisn,jink->bkdjs", filtered, dft_matrix(), precision=highest)
    spectra = spectra.reshape(CHANNELS, DISHES, 2, spectra_total)

    def per_channel(operands):
        channel_spec, channel_phase = operands
        left_side = channel_spec.reshape(DISHES, 2 * spectra_total)
        swapped = jnp.concatenate([-channel_spec[:, 1], channel_spec[:, 0]], axis=-1)
        right_side = jnp.stack([left_side, swapped])
        visible = jnp.einsum("rk,vqk->vrq", left_side, right_side, precision=highest) / spectra_total
        steer_angle = channel_phase.astype(jnp.float32) * (2.0 * math.pi / PHASE_LEVELS)
        cosine = jnp.cos(steer_angle)
        sine = jnp.sin(steer_angle)
        gains = jnp.stack([jnp.stack([cosine, sine], -1), jnp.stack([-sine, cosine], -1)])
        beams = jnp.einsum("vbri,ris->vbs", gains, channel_spec, precision=highest)
        power_out = (beams[0] * beams[0] + beams[1] * beams[1]) / DISHES
        return visible, power_out

    visibilities, beam_power = lax.map(per_channel, (spectra, phases))
    return visibilities, beam_power
```

```python
import functools
import math

import jax
import jax.numpy as jnp
import numpy as np
from jax import lax
from jax.experimental import pallas as pl
from jax.experimental.pallas import tpu as pltpu
from jax.sharding import PartitionSpec as P

PHASE_LEVELS = 256
LANES = 128

f32 = jnp.float32
bf16 = jnp.bfloat16
VMEM = pltpu.VMEM
NT = (((1,), (1,)), ((), ()))
NN = (((1,), (0,)), ((), ()))


def split(x):
    hi = x.astype(bf16)
    return hi, (x - hi.astype(f32)).astype(bf16)


def dot3(a, b, dims):
    mm = functools.partial(lax.dot_general, dimension_numbers=dims, preferred_element_type=f32)
    return mm(a[0], b[0]) + (mm(a[0], b[1]) + mm(a[1], b[0]))


def twiddle_table(fine, per_section):
    n = np.arange(LANES) % fine
    ch = np.arange(fine)
    angle = 2.0 * math.pi * (np.outer(ch, n) % fine) / fine
    cos, sin = np.cos(angle), np.sin(angle)
    table = np.stack([np.stack([cos, -sin], 1), np.stack([sin, cos], 1)], 0)
    table = table.reshape(2, fine // per_section, per_section * 2, LANES)
    return np.ascontiguousarray(table.transpose(1, 0, 2, 3)).astype(np.float32)


def filter_kernel(geom, where, x_ref, table_ref, taps_ref, *rest):
    dishes, coarse, sections, rows4, u_count, j_count, spec_rows, row_count = geom
    outs, (coef, coef_hi, coef_lo) = rest[:-3], rest[-3:]
    me = where[0]
    slot = me % sections
    band0 = me // sections
    half = sections * rows4
    for kc in range(sections):
        for i in range(2):
            base = table_ref[slot ^ kc, i]
            for u in range(u_count):
                for j in range(j_count):
                    c = i * j_count + j
                    row = u * j_count + j
                    coef[u * half + kc * rows4 : u * half + (kc + 1) * rows4, c * LANES : (c + 1) * LANES] = (
                        base * taps_ref[row : row + 1, :]
                    )
    coef_hi[...], coef_lo[...] = split(coef[...])

    group = u_count
    lane = lax.broadcasted_iota(jnp.int32, (8, LANES), 1)
    sub = lax.broadcasted_iota(jnp.int32, (8, LANES), 0)
    low_lane, low_sub = lane < spec_rows, sub < 4
    for kb in range(coarse):
        band = band0 ^ kb

        def step(dg, carry):
            pieces = []
            for d in range(group):
                start = ((dg * group + d) * coarse + band) * row_count
                pieces.append(
                    jnp.concatenate(
                        [
                            x_ref[pl.ds(start * 2 + 2 * j + i, spec_rows, stride=2), :]
                            for i in range(2)
                            for j in range(j_count)
                        ],
                        axis=1,
                    )
                )
            x = split(jnp.concatenate(pieces, axis=0))
            out = dot3((coef_hi[...], coef_lo[...]), x, NT)
            per_tile = 8 // rows4
            for g in range(half // 8):
                for u1 in range(2):
                    tiles = []
                    for d1 in range(2):
                        a0, a1 = (
                            out[
                                (u1 * 2 + u0) * half + g * 8 : (u1 * 2 + u0) * half + g * 8 + 8,
                                d1 * LANES : (d1 + 1) * LANES,
                            ]
                            for u0 in range(2)
                        )
                        tiles.append(jnp.where(low_lane, a0, pltpu.roll(a1, spec_rows, 1)))
                        tiles.append(jnp.where(low_lane, pltpu.roll(a0, spec_rows, 1), a1))
                    for t in range(0, group, per_tile):
                        at = pl.multiple_of((dg * group + t) * rows4, 8)
                        for kk in range(per_tile):
                            k = kb * sections + per_tile * g + kk
                            if per_tile == 2:
                                b0, b1 = tiles[t], tiles[t + 1]
                                if kk == 0:
                                    tile = jnp.where(low_sub, b0, pltpu.roll(b1, 4, 0))
                                else:
                                    tile = jnp.where(low_sub, pltpu.roll(b0, 4, 0), b1)
                            else:
                                tile = jnp.concatenate(
                                    [b[kk * rows4 : (kk + 1) * rows4] for b in tiles[t : t + per_tile]], axis=0
                                )
                            outs[k][u1, pl.ds(at, 8), :] = tile
            return carry

        lax.fori_loop(0, dishes // group, step, 0)


def filter_bank(where, voltages, filter_taps, n):
    _, dishes, coarse, parts, samples = voltages.shape
    taps, fine = filter_taps.shape
    spectra = samples // fine - taps + 1
    per_section = coarse * fine // n
    sections = fine // per_section
    u_count = LANES // fine
    j_count = -(-(u_count - 1 + taps) * fine // LANES)
    spec_rows = spectra // u_count
    row_count = spec_rows + j_count - 1
    rows4 = per_section * 2
    assert u_count == 4 and spec_rows == 64 and rows4 in (2, 4) and dishes % 4 == 0
    x = jnp.pad(voltages[0], ((0, 0), (0, 0), (0, 0), (0, row_count * LANES - samples)))
    x = x.reshape(dishes, coarse, parts, row_count, LANES).transpose(0, 1, 3, 2, 4)
    x = x.reshape(dishes * coarse * row_count * parts, LANES)
    flat = filter_taps.reshape(-1)
    shifted = [
        jnp.pad(flat, (u * fine, j_count * LANES - taps * fine - u * fine)) for u in range(u_count)
    ]
    taps_rows = jnp.stack(shifted).reshape(u_count * j_count, LANES)
    geom = (dishes, coarse, sections, rows4, u_count, j_count, spec_rows, row_count)
    width = 2 * j_count * LANES
    rows = u_count * sections * rows4
    block = jax.ShapeDtypeStruct((spectra // LANES, dishes * rows4, LANES), f32)
    return pl.pallas_call(
        functools.partial(filter_kernel, geom),
        grid_spec=pltpu.PrefetchScalarGridSpec(
            num_scalar_prefetch=1,
            grid=(1,),
            in_specs=[pl.BlockSpec(memory_space=VMEM)] * 3,
            out_specs=[pl.BlockSpec(memory_space=VMEM)] * n,
            scratch_shapes=[VMEM((rows, width), f32), VMEM((rows, width), bf16), VMEM((rows, width), bf16)],
        ),
        out_shape=[block] * n,
        compiler_params=pltpu.CompilerParams(vmem_limit_bytes=12 << 20),
        cost_estimate=pl.CostEstimate(
            flops=6 * rows * width * dishes * coarse * spec_rows, bytes_accessed=5 << 20, transcendentals=0
        ),
        name="filter_bank",
    )(where, x, jnp.asarray(twiddle_table(fine, per_section)), taps_rows)


def gain_kernel(where, phase_ref, hi_ref, lo_ref):
    beams = phase_ref.shape[1]
    level = phase_ref[0]
    quarter = PHASE_LEVELS // 4
    turn = (level + quarter // 2) // quarter
    x = (level - turn * quarter).astype(f32) * (2.0 * math.pi / PHASE_LEVELS)
    x2 = x * x
    sin = x + x * x2 * (-1.0 / 6 + x2 * (1.0 / 120 + x2 * (-1.0 / 5040 + x2 * (1.0 / 362880))))
    cos = 1.0 + x2 * (-0.5 + x2 * (1.0 / 24 + x2 * (-1.0 / 720 + x2 * (1.0 / 40320 - x2 * (1.0 / 3628800)))))
    odd = (turn & 1) == 1
    c = jnp.where(odd, sin, cos)
    s = jnp.where(odd, cos, sin)
    c = jnp.where(((turn + 1) & 2) == 2, -c, c)
    s = jnp.where((turn & 2) == 2, -s, s)
    hi_ref[0, :beams], lo_ref[0, :beams] = split(c)
    hi_ref[0, beams:], lo_ref[0, beams:] = split(s)


def gains(where, phases, beams, local, name):
    channels, _, dishes = phases.shape
    out = jax.ShapeDtypeStruct((channels, 2 * beams, dishes), bf16)
    whole = pl.BlockSpec((1, 2 * beams, dishes), lambda p, w: (p, 0, 0))
    return pl.pallas_call(
        gain_kernel,
        grid_spec=pltpu.PrefetchScalarGridSpec(
            num_scalar_prefetch=1,
            grid=(channels,),
            in_specs=[pl.BlockSpec((1, beams, dishes), lambda p, w: (p, w[1] if local else 0, 0))],
            out_specs=[whole, whole],
        ),
        out_shape=[out, out],
        compiler_params=pltpu.CompilerParams(vmem_limit_bytes=16 << 20),
        cost_estimate=pl.CostEstimate(
            flops=40 * channels * beams * dishes, bytes_accessed=12 * channels * beams * dishes, transcendentals=0
        ),
        name=name,
    )(where, phases)


def unpack(blocks, ks, where, base, hi, lo, dishes):
    channels, _, width = hi.shape
    spectra = width // 2
    pair = 1 if dishes % 16 == 0 else 16 // dishes
    assert pair <= 2
    blocks = list(blocks)
    for first in range(0, len(blocks), pair):
        at = pl.multiple_of(base(ks[first]) // pair * pair * dishes, pair * dishes)
        flip = (base(ks[first]) % pair) == 1
        for p in range(channels):
            for part in range(2):
                for u in range(spectra // LANES):
                    got = [
                        block[u, pl.ds(p * 2 + part, dishes, stride=channels * 2), :]
                        for block in blocks[first : first + pair]
                    ]
                    if pair == 2:
                        a, b = got
                        got = [jnp.where(flip, b, a), jnp.where(flip, a, b)]
                    h, l = split(jnp.concatenate(got, axis=0))
                    col = part * spectra + u * LANES
                    hi[p, pl.ds(at, pair * dishes), col : col + LANES] = h
                    lo[p, pl.ds(at, pair * dishes), col : col + LANES] = l


def correlate(v_ref, left, right, spectra):
    scale = 1.0 / spectra
    turned = tuple(jnp.concatenate([-r[:, spectra:], r[:, :spectra]], axis=1) for r in right)
    v_ref[0, 0] = dot3(left, right, NT) * scale
    v_ref[0, 1] = dot3(left, turned, NT) * scale


def own_kernel(n, dishes, where, *refs):
    blocks, (ghi, glo, v_ref, q_ref, xhi, xlo) = refs[:n], refs[n:]
    p, cb = pl.program_id(0), pl.program_id(1)
    me = where[0]

    @pl.when((p == 0) & (cb == 0))
    def _():
        unpack(blocks, range(n), where, lambda k: me ^ k, xhi, xlo, dishes)

    @pl.when(cb == 0)
    def _():
        q_ref[0] = dot3((ghi[p], glo[p]), (xhi[p], xlo[p]), NN)

    cols = v_ref.shape[3]
    at = pl.ds(pl.multiple_of(cb * cols, cols), cols)
    correlate(v_ref, (xhi[p], xlo[p]), (xhi[p, at, :], xlo[p, at, :]), xhi.shape[2] // 2)


def other_kernel(n, dishes, part, last, where, *refs):
    per = len(range(n)) // 2
    blocks, refs = refs[:per], refs[per:]
    xhi, xlo, ghi, glo, q_in = refs[:5]
    v_ref, q_ref, ohi, olo = refs[-4:]
    p = pl.program_id(0)
    me = where[0]
    ks = range(part * per, (part + 1) * per)

    @pl.when(p == 0)
    def _():
        unpack(blocks, ks, where, lambda k: (me ^ k) % per, ohi, olo, dishes)

    spectra = xhi.shape[2] // 2
    correlate(v_ref, (xhi[p], xlo[p]), (ohi[p], olo[p]), spectra)
    cols = per * dishes
    q = q_in[0] + dot3((ghi[0], glo[0]), (ohi[p], olo[p]), NN)
    if not last:
        q_ref[0] = q
        return
    beams = q.shape[0] // 2
    re = q[:beams, :spectra] + q[beams:, spectra:]
    im = q[:beams, spectra:] - q[beams:, :spectra]
    power = (re * re + im * im) * (1.0 / (2 * n * dishes))
    u_count = 4
    rows = spectra // u_count
    got = lax.broadcasted_iota(jnp.int32, (spectra, spectra), 0)
    want = lax.broadcasted_iota(jnp.int32, (spectra, spectra), 1)
    pick = ((got % rows) * u_count + got // rows == want).astype(bf16)
    total = jnp.zeros_like(power)
    for _ in range(3):
        piece = power.astype(bf16)
        total += lax.dot_general(piece, pick, NN, preferred_element_type=f32)
        power = power - piece.astype(f32)
    q_ref[0] = total


def per_device(n, n_quad, voltages, filter_taps, phases):
    dishes = voltages.shape[1]
    channels, beams_all, section = phases.shape
    beams = beams_all // n_quad
    me = lax.axis_index("chan").astype(jnp.int32)
    quad = lax.axis_index("quad").astype(jnp.int32)
    where = jnp.stack([me, quad])
    swap = [(0, 1), (1, 0)]

    with jax.named_scope("phase_swap"):
        theirs = lax.dynamic_slice_in_dim(phases, (1 - quad) * beams, beams, 1)
        received = lax.ppermute(theirs, "quad", swap)

    with jax.named_scope("filter"):
        sent = filter_bank(where, voltages, filter_taps, n)
    spectra = sent[0].shape[0] * LANES

    own = []
    for k in range(n):
        with jax.named_scope(f"turn_{k}"):
            own.append(lax.ppermute(sent[k], "chan", [(i, i ^ k) for i in range(n)]) if k else sent[k])
    other = []
    for k in range(n):
        with jax.named_scope(f"cross_{k}"):
            other.append(lax.ppermute(own[k], "quad", swap))

    own_hi, own_lo = gains(where, phases, beams, True, "gains_own")
    oth_hi, oth_lo = gains(where, received, beams, False, "gains_other")

    rows = n * dishes
    cols = rows // 2
    vis_shape = jax.ShapeDtypeStruct((channels, 2, rows, n_quad * rows), f32)
    q_shape = jax.ShapeDtypeStruct((channels, 2 * beams, 2 * spectra), f32)
    x_shape = jax.ShapeDtypeStruct((channels, rows, 2 * spectra), bf16)
    whole = pl.BlockSpec(memory_space=VMEM)
    mm = 3 * 2 * rows * cols * 2 * spectra * channels
    vis, q, xhi, xlo = pl.pallas_call(
        functools.partial(own_kernel, n, dishes),
        grid_spec=pltpu.PrefetchScalarGridSpec(
            num_scalar_prefetch=1,
            grid=(channels, 2),
            in_specs=[whole] * (n + 2),
            out_specs=[
                pl.BlockSpec((1, 2, rows, cols), lambda p, cb, w: (p, 0, 0, w[1] * 2 + cb)),
                pl.BlockSpec((1, 2 * beams, 2 * spectra), lambda p, cb, w: (p, 0, 0)),
                whole,
                whole,
            ],
        ),
        out_shape=[vis_shape, q_shape, x_shape, x_shape],
        compiler_params=pltpu.CompilerParams(vmem_limit_bytes=24 << 20),
        cost_estimate=pl.CostEstimate(flops=6 * mm, bytes_accessed=12 << 20, transcendentals=0),
        name="own_products",
    )(where, *own, own_hi, own_lo)

    per = n // 2
    for part in range(2):
        last = part == 1
        col_block = functools.partial(lambda part, p, w: (p, 0, 0, (1 - w[1]) * 2 + ((w[0] // per) ^ part)), part)
        g_block = pl.BlockSpec(
            (1, 2 * beams, cols), functools.partial(lambda part, p, w: (p, 0, (w[0] // per) ^ part), part)
        )
        q_block = pl.BlockSpec((1, 2 * beams, 2 * spectra), lambda p, w: (p, 0, 0))
        p_block = pl.BlockSpec((1, beams, spectra), lambda p, w: (p, 0, 0))
        vis, q = pl.pallas_call(
            functools.partial(other_kernel, n, dishes, part, last),
            grid_spec=pltpu.PrefetchScalarGridSpec(
                num_scalar_prefetch=1,
                grid=(channels,),
                in_specs=[whole] * per + [whole, whole, g_block, g_block, q_block, pl.BlockSpec(memory_space=pl.ANY)],
                out_specs=[pl.BlockSpec((1, 2, rows, cols), col_block), p_block if last else q_block],
                scratch_shapes=[VMEM((channels, cols, 2 * spectra), bf16)] * 2,
            ),
            out_shape=[vis_shape, jax.ShapeDtypeStruct((channels, beams, spectra), f32) if last else q_shape],
            input_output_aliases={1 + per + 5: 0},
            compiler_params=pltpu.CompilerParams(vmem_limit_bytes=24 << 20),
            cost_estimate=pl.CostEstimate(flops=3 * mm, bytes_accessed=8 << 20, transcendentals=0),
            name=f"other_products_{part}",
        )(where, *other[part * per : (part + 1) * per], xhi, xlo, oth_hi, oth_lo, q, vis)
    return vis, q


def solution(mesh):
    n, n_quad = mesh.shape["chan"], mesh.shape["quad"]
    assert n_quad == 2 and n & (n - 1) == 0
    return jax.shard_map(
        functools.partial(per_device, n, n_quad),
        mesh=mesh,
        in_specs=(P("quad", "chan", None, None, None), P(), P("chan", None, "quad")),
        out_specs=(P("chan", None, "quad", None), P("chan", "quad", None)),
        check_vma=False,
    )
```

```python
import functools
import math

import jax
import jax.numpy as jnp
import numpy as np
from jax import lax
from jax.experimental import pallas as pl
from jax.experimental.pallas import tpu as pltpu
from jax.sharding import PartitionSpec as P


PHASE_LEVELS = 256
LANES = 128

f32 = jnp.float32
bf16 = jnp.bfloat16
VMEM = pltpu.VMEM
NT = (((1,), (1,)), ((), ()))
NN = (((1,), (0,)), ((), ()))


def split(x):
    hi = x.astype(bf16)
    return hi, (x - hi.astype(f32)).astype(bf16)


def dot3(a, b, dims):
    mm = functools.partial(lax.dot_general, dimension_numbers=dims, preferred_element_type=f32)
    return mm(a[0], b[0]) + (mm(a[0], b[1]) + mm(a[1], b[0]))


SHIFTS = (0, 1, 3, 2)


def partner(me, size, k, sign):
    z, low = me // size, me % size
    at = ((z ^ (z >> 1)) + 4 + sign * SHIFTS[k // size]) % 4
    return (at ^ (at >> 1)) * size + (low ^ (k % size))


def twiddle_table(fine, per_section):
    n = np.arange(LANES) % fine
    ch = np.arange(fine)
    angle = 2.0 * math.pi * (np.outer(ch, n) % fine) / fine
    cos, sin = np.cos(angle), np.sin(angle)
    table = np.stack([np.stack([cos, -sin], 1), np.stack([sin, cos], 1)], 0)
    table = table.reshape(2, fine // per_section, per_section * 2, LANES)
    return np.ascontiguousarray(table.transpose(1, 0, 2, 3)).astype(np.float32)


def filter_kernel(geom, where, x_ref, table_ref, taps_ref, *rest):
    dishes, coarse, sections, rows4, u_count, j_count, spec_rows, row_count, n = geom
    outs, (coef, coef_hi, coef_lo) = rest[:-3], rest[-3:]
    me = where[0]
    size = n // 4
    chunk = n if coarse == 1 else size
    half = chunk * rows4
    for k in range(n):
        top, kc = k // chunk * u_count * half, k % chunk
        for i in range(2):
            base = table_ref[partner(me, size, k, 1) % sections, i]
            for u in range(u_count):
                for j in range(j_count):
                    c = i * j_count + j
                    row = u * j_count + j
                    coef[top + u * half + kc * rows4 : top + u * half + (kc + 1) * rows4, c * LANES : (c + 1) * LANES] = (
                        base * taps_ref[row : row + 1, :]
                    )
    coef_hi[...], coef_lo[...] = split(coef[...])

    group = u_count
    lane = lax.broadcasted_iota(jnp.int32, (8, LANES), 1)
    sub = lax.broadcasted_iota(jnp.int32, (8, LANES), 0)
    low_lane, low_sub = lane < spec_rows, sub < 4
    for kb in range(n // chunk):
        band = partner(me, size, kb * chunk, 1) // sections if coarse > 1 else 0
        mine = slice(kb * u_count * half, (kb + 1) * u_count * half)

        def step(dg, carry):
            pieces = []
            for d in range(group):
                start = ((dg * group + d) * coarse + band) * row_count * 2
                pieces.append(
                    jnp.concatenate(
                        [
                            x_ref[pl.ds(start + j * 2 + i, spec_rows, stride=2), :]
                            for i in range(2)
                            for j in range(j_count)
                        ],
                        axis=1,
                    )
                )
            x = split(jnp.concatenate(pieces, axis=0))
            out = dot3((coef_hi[mine, :], coef_lo[mine, :]), x, NT)
            per_tile = 8 // rows4
            for g in range(half // 8):
                for u1 in range(2):
                    tiles = []
                    for d1 in range(2):
                        a0, a1 = (
                            out[
                                (u1 * 2 + u0) * half + g * 8 : (u1 * 2 + u0) * half + g * 8 + 8,
                                d1 * LANES : (d1 + 1) * LANES,
                            ]
                            for u0 in range(2)
                        )
                        tiles.append(jnp.where(low_lane, a0, pltpu.roll(a1, spec_rows, 1)))
                        tiles.append(jnp.where(low_lane, pltpu.roll(a0, spec_rows, 1), a1))
                    for t in range(0, group, per_tile):
                        at = pl.multiple_of((dg * group + t) * rows4, 8)
                        for kk in range(per_tile):
                            k = kb * chunk + per_tile * g + kk
                            if per_tile == 2:
                                b0, b1 = tiles[t], tiles[t + 1]
                                if kk == 0:
                                    tile = jnp.where(low_sub, b0, pltpu.roll(b1, 4, 0))
                                else:
                                    tile = jnp.where(low_sub, pltpu.roll(b0, 4, 0), b1)
                            else:
                                tile = jnp.concatenate(
                                    [b[kk * rows4 : (kk + 1) * rows4] for b in tiles[t : t + per_tile]], axis=0
                                )
                            outs[k][u1, pl.ds(at, 8), :] = tile
            return carry

        lax.fori_loop(0, dishes // group, step, 0)


def rows_kernel(samples, x_ref, out_ref):
    full, tail = samples // LANES, samples % LANES

    def step(d, carry):
        for r in range(full):
            out_ref[d, :, r] = x_ref[0, d, :, :, r * LANES : (r + 1) * LANES]
        if tail:
            out_ref[d, :, full] = jnp.zeros(out_ref.shape[1:2] + out_ref.shape[3:], f32)
            out_ref[d, :, full, :, :tail] = x_ref[0, d, :, :, full * LANES :]
        return carry

    lax.fori_loop(0, x_ref.shape[1], step, 0)


def filter_bank(where, voltages, filter_taps, n):
    _, dishes, coarse, parts, samples = voltages.shape
    taps, fine = filter_taps.shape
    spectra = samples // fine - taps + 1
    per_section = coarse * fine // n
    sections = fine // per_section
    u_count = LANES // fine
    j_count = -(-(u_count - 1 + taps) * fine // LANES)
    spec_rows = spectra // u_count
    row_count = spec_rows + j_count - 1
    rows4 = per_section * 2
    assert u_count == 4 and spec_rows == 64 and rows4 in (2, 4) and dishes % 4 == 0
    x = pl.pallas_call(
        functools.partial(rows_kernel, samples),
        in_specs=[pl.BlockSpec(memory_space=VMEM)],
        out_specs=pl.BlockSpec(memory_space=VMEM),
        out_shape=jax.ShapeDtypeStruct((dishes, coarse, row_count, parts, LANES), f32),
        compiler_params=pltpu.CompilerParams(vmem_limit_bytes=1 << 20),
        cost_estimate=pl.CostEstimate(flops=0, bytes_accessed=4 << 20, transcendentals=0),
        name="rows",
    )(voltages)
    x = x.reshape(dishes * coarse * row_count * parts, LANES)
    flat = filter_taps.reshape(-1)
    shifted = [
        jnp.pad(flat, (u * fine, j_count * LANES - taps * fine - u * fine)) for u in range(u_count)
    ]
    taps_rows = jnp.stack(shifted).reshape(u_count * j_count, LANES)
    geom = (dishes, coarse, sections, rows4, u_count, j_count, spec_rows, row_count, n)
    width = 2 * j_count * LANES
    rows = u_count * n * rows4
    block = jax.ShapeDtypeStruct((spectra // LANES, dishes * rows4, LANES), f32)
    return pl.pallas_call(
        functools.partial(filter_kernel, geom),
        grid_spec=pltpu.PrefetchScalarGridSpec(
            num_scalar_prefetch=1,
            grid=(1,),
            in_specs=[pl.BlockSpec(memory_space=VMEM)] * 3,
            out_specs=[pl.BlockSpec(memory_space=VMEM)] * n,
            scratch_shapes=[VMEM((rows, width), f32), VMEM((rows, width), bf16), VMEM((rows, width), bf16)],
        ),
        out_shape=[block] * n,
        compiler_params=pltpu.CompilerParams(vmem_limit_bytes=12 << 20),
        cost_estimate=pl.CostEstimate(
            flops=6 * rows * width * dishes * spec_rows, bytes_accessed=5 << 20, transcendentals=0
        ),
        name="filter_bank",
    )(where, x, jnp.asarray(twiddle_table(fine, per_section)), taps_rows)


def gain_kernel(where, phase_ref, hi_ref, lo_ref):
    beams = phase_ref.shape[1]
    level = phase_ref[0]
    quarter = PHASE_LEVELS // 4
    turn = (level + quarter // 2) // quarter
    x = (level - turn * quarter).astype(f32) * (2.0 * math.pi / PHASE_LEVELS)
    x2 = x * x
    sin = x + x * x2 * (-1.0 / 6 + x2 * (1.0 / 120 + x2 * (-1.0 / 5040 + x2 * (1.0 / 362880))))
    cos = 1.0 + x2 * (-0.5 + x2 * (1.0 / 24 + x2 * (-1.0 / 720 + x2 * (1.0 / 40320 - x2 * (1.0 / 3628800)))))
    odd = (turn & 1) == 1
    c = jnp.where(odd, sin, cos)
    s = jnp.where(odd, cos, sin)
    c = jnp.where(((turn + 1) & 2) == 2, -c, c)
    s = jnp.where((turn & 2) == 2, -s, s)
    hi_ref[0, :beams], lo_ref[0, :beams] = split(c)
    hi_ref[0, beams:], lo_ref[0, beams:] = split(s)


def gains(where, phases, beams, local):
    channels, _, dishes = phases.shape
    out = jax.ShapeDtypeStruct((channels, 2 * beams, dishes), bf16)
    whole = pl.BlockSpec((1, 2 * beams, dishes), lambda p, w: (p, 0, 0))
    return pl.pallas_call(
        gain_kernel,
        grid_spec=pltpu.PrefetchScalarGridSpec(
            num_scalar_prefetch=1,
            grid=(channels,),
            in_specs=[pl.BlockSpec((1, beams, dishes), lambda p, w: (p, w[1] if local else 0, 0))],
            out_specs=[whole, whole],
        ),
        out_shape=[out, out],
        compiler_params=pltpu.CompilerParams(vmem_limit_bytes=(48 if local else 16) << 20),
        cost_estimate=pl.CostEstimate(
            flops=40 * channels * beams * dishes, bytes_accessed=12 * channels * beams * dishes, transcendentals=0
        ),
    )(where, phases)


def put(hi, lo, p, at, rows, col, value):
    h, l = split(value)
    hi[p, pl.ds(at, rows), col : col + value.shape[1]] = h
    lo[p, pl.ds(at, rows), col : col + value.shape[1]] = l


def unpack(blocks, first, me, base, dishes, hi, lo, full):
    channels, _, width = hi.shape
    spectra = width // 2
    count = len(blocks)
    pair = 1 if dishes % 16 == 0 else 16 // dishes
    assert pair <= 2
    rows = pair * dishes
    flip = (me % 2) == 1
    for b in range(0, count, pair):
        place = ((me ^ (first + b)) % count) // pair * rows
        for p in range(channels):
            for part in range(2):
                for u in range(spectra // LANES):
                    got = [
                        block[u, pl.ds(p * 2 + part, dishes, stride=channels * 2), :] for block in blocks[b : b + pair]
                    ]
                    if pair == 2:
                        got = [jnp.where(flip, got[1], got[0]), jnp.where(flip, got[0], got[1])]
                    value = jnp.concatenate(got, axis=0)
                    col = part * spectra + u * LANES
                    put(hi, lo, p, pl.multiple_of(base + place, rows), rows, col, value)
                    if full is not None:
                        full[p, pl.ds(pl.multiple_of(place, rows), rows), col : col + LANES] = value


def own_group_kernel(geom, group, where, *refs):
    _, dishes = geom
    size = LANES // dishes
    blocks = refs[:size]
    outs = refs[size:] if group % 2 == 0 else refs[size + 2 :]
    hi, lo = outs[:2]
    full = outs[2] if len(outs) > 2 else None
    me = where[0]
    base = group % 2 * LANES
    unpack(blocks, group * size, me, base, dishes, hi, lo, full)


def own_group(geom, where, group, blocks, pair, channels, spectra, send):
    half = jax.ShapeDtypeStruct((channels, 2 * LANES, 2 * spectra), bf16)
    full = jax.ShapeDtypeStruct((channels, LANES, 2 * spectra), f32)
    whole = pl.BlockSpec(memory_space=VMEM)
    out = [half, half] + ([full] if send else [])
    at = 1 + len(blocks)
    return pl.pallas_call(
        functools.partial(own_group_kernel, geom, group),
        grid_spec=pltpu.PrefetchScalarGridSpec(
            num_scalar_prefetch=1,
            grid=(1,),
            in_specs=[whole] * (len(blocks) + len(pair)),
            out_specs=[whole] * len(out),
        ),
        out_shape=out,
        input_output_aliases={at: 0, at + 1: 1} if pair else {},
        compiler_params=pltpu.CompilerParams(vmem_limit_bytes=2 << 20),
        cost_estimate=pl.CostEstimate(flops=1 << 20, bytes_accessed=2 << 20, transcendentals=0),
    )(where, *blocks, *pair)


def turned(x):
    half = x.shape[1] // 2
    return jnp.concatenate([-x[:, half:], x[:, :half]], axis=1)


def beam_terms(g_hi, g_lo, p, ats, x):
    hi, lo = ([g[p, :, pl.ds(pl.multiple_of(at, LANES), LANES)] for at in ats] for g in (g_hi, g_lo))
    left = jnp.concatenate(hi + hi + lo, axis=1)
    right = jnp.concatenate([x[0], x[1], x[0]], axis=0)
    return lax.dot_general(left, right, NN, preferred_element_type=f32)


class Writer:
    def __init__(self, vis, stage, sems, scale):
        self.vis, self.stage, self.sems, self.scale = vis, stage, sems, scale
        self.slots, self.copies = 0, []

    def put(self, p, v, rows, cols, value):
        slot = self.slots
        self.slots += 1
        self.stage[slot] = value * self.scale
        for i, row in enumerate(rows):
            for j, col in enumerate(cols):
                source = self.stage.at[slot, i * LANES : (i + 1) * LANES, j * LANES : (j + 1) * LANES]
                target = self.vis.at[
                    p, v, pl.ds(pl.multiple_of(row, LANES), LANES), pl.ds(pl.multiple_of(col, LANES), LANES)
                ]
                copy = pltpu.make_async_copy(source, target, self.sems.at[len(self.copies)])
                copy.start()
                self.copies.append(copy)

    def wide(self, p, rows, cols, left, right):
        self.put(p, 0, rows, cols, dot3(left, right, NT))
        self.put(p, 1, rows, cols, dot3(left, tuple(turned(r) for r in right), NT))

    def narrow(self, p, rows, cols, left, right):
        both = dot3(left, tuple(jnp.concatenate([r, turned(r)], axis=0) for r in right), NT)
        width = right[0].shape[0]
        self.put(p, 0, rows, cols, both[:, :width])
        self.put(p, 1, rows, cols, both[:, width:])

    def finish(self):
        for copy in self.copies:
            copy.wait()


def places(geom, where):
    n, dishes = geom
    size = LANES // dishes
    at = [partner(where[0], size, g * size, -1) // size * LANES for g in range(4)]
    total = n * dishes
    return at, where[1] * total, (1 - where[1]) * total


def first_kernel(geom, where, *refs):
    own_hi, own_lo, far0, far1, gho, glo, ghf, glf, vis, q_ref, far_hi, far_lo, stage, sems = refs
    channels, _, width = own_hi.shape
    at, here, there = places(geom, where)
    near = at[:2]
    out = Writer(vis, stage, sems, 2.0 / width)
    for p in range(channels):
        for g, far in enumerate((far0, far1)):
            put(far_hi, far_lo, p, g * LANES, LANES, 0, far[p])
        mine, theirs = (own_hi[p], own_lo[p]), (far_hi[p], far_lo[p])
        out.wide(p, near, [here + a for a in near], mine, mine)
        out.wide(p, near, [there + a for a in near], mine, theirs)
        q_ref[p] = beam_terms(gho, glo, p, near, mine) + beam_terms(ghf, glf, p, near, theirs)
    out.finish()


def second_kernel(geom, where, *refs):
    near_hi, near_lo, own_hi, own_lo, far_hi, far_lo, gho, glo, q_in, _, vis, q_ref, stage, sems = refs
    channels, _, width = own_hi.shape
    at, here, there = places(geom, where)
    near, away = at[:2], at[2:]
    out = Writer(vis, stage, sems, 2.0 / width)
    for p in range(channels):
        first, mine, theirs = (near_hi[p], near_lo[p]), (own_hi[p], own_lo[p]), (far_hi[p], far_lo[p])
        out.wide(p, away, [here + a for a in away], mine, mine)
        out.wide(p, away, [here + a for a in near], mine, first)
        out.wide(p, near, [here + a for a in away], first, mine)
        out.wide(p, away, [there + a for a in near], mine, theirs)
        q_ref[p] = q_in[p] + beam_terms(gho, glo, p, away, mine)
    out.finish()


def late_kernel(geom, group, raw, where, *refs):
    n, dishes = geom
    size = LANES // dishes
    got, refs = refs[: size if raw else 1], refs[size if raw else 1 :]
    near_hi, near_lo, own_hi, own_lo, ghf, glf, q_in, _, vis, q_ref, stage, sems = refs[:12]
    hi, lo = refs[12:]
    channels, _, width = own_hi.shape
    at, _, there = places(geom, where)
    col = there + at[group]
    if raw:
        unpack(got, group * size, where[0], 0, dishes, hi, lo, None)
    out = Writer(vis, stage, sems, 2.0 / width)
    for p in range(channels):
        if not raw:
            put(hi, lo, p, 0, LANES, 0, got[0][p])
        x = (hi[p], lo[p])
        out.narrow(p, at[:2], [col], (near_hi[p], near_lo[p]), x)
        out.narrow(p, at[2:], [col], (own_hi[p], own_lo[p]), x)
    for p in range(channels):
        q = q_in[p] + beam_terms(ghf, glf, p, [at[group]], (hi[p], lo[p]))
        if not raw:
            q_ref[p] = q
            continue
        beams, spectra = q.shape[0] // 2, q.shape[1] // 2
        re = q[:beams, :spectra] + q[beams:, spectra:]
        im = q[:beams, spectra:] - q[beams:, :spectra]
        power = (re * re + im * im) * (1.0 / (2 * n * dishes))
        u_count = spectra // 64
        got_at = lax.broadcasted_iota(jnp.int32, (spectra, spectra), 0)
        want_at = lax.broadcasted_iota(jnp.int32, (spectra, spectra), 1)
        pick = ((got_at % 64) * u_count + got_at // 64 == want_at).astype(bf16)
        ordered = jnp.zeros_like(power)
        for _ in range(3):
            piece = power.astype(bf16)
            ordered += lax.dot_general(piece, pick, NN, preferred_element_type=f32)
            power = power - piece.astype(f32)
        q_ref[p] = ordered
    out.finish()


def products(kernel, where, ins, outs, aliases, slots, block, more, flops):
    whole, where_it_is = pl.BlockSpec(memory_space=VMEM), pl.BlockSpec(memory_space=pl.ANY)
    vis_shape = outs[0].shape
    return pl.pallas_call(
        kernel,
        grid_spec=pltpu.PrefetchScalarGridSpec(
            num_scalar_prefetch=1,
            grid=(1,),
            in_specs=[where_it_is if x.shape == vis_shape else whole for x in ins],
            out_specs=[where_it_is] + [whole] * (len(outs) - 1),
            scratch_shapes=[VMEM((slots,) + block, f32), pltpu.SemaphoreType.DMA((4 * slots,))] + more,
        ),
        out_shape=outs,
        input_output_aliases={1 + i: o for i, o in aliases.items()},
        compiler_params=pltpu.CompilerParams(vmem_limit_bytes=16 << 20),
        cost_estimate=pl.CostEstimate(flops=flops, bytes_accessed=4 << 20, transcendentals=0),
    )(where, *ins)


def phase_kernel(where, phases, out, sems):
    channels, beams, _ = out.shape
    pieces = sems.shape[0] // channels
    rows = beams // pieces
    at = (1 - where[1]) * beams
    copies = []
    for p in range(channels):
        for i in range(pieces):
            copies.append(
                pltpu.make_async_copy(
                    phases.at[p, pl.ds(pl.multiple_of(at + i * rows, rows), rows), :],
                    out.at[p, i * rows : (i + 1) * rows, :],
                    sems.at[p * pieces + i],
                )
            )
    for copy in copies:
        copy.start()
    for copy in copies:
        copy.wait()


def per_device(n, n_quad, voltages, filter_taps, phases):
    return whole_step(n, n_quad, voltages, filter_taps, phases)


def whole_step(n, n_quad, voltages, filter_taps, phases):
    dishes = voltages.shape[1]
    channels, beams_all, _ = phases.shape
    beams = beams_all // n_quad
    size = LANES // dishes
    groups = n // size
    assert groups == 4
    geom = (n, dishes)
    me = lax.axis_index("chan").astype(jnp.int32)
    quad = lax.axis_index("quad").astype(jnp.int32)
    where = jnp.stack([me, quad])
    swap = [(0, 1), (1, 0)]

    theirs = pl.pallas_call(
        phase_kernel,
        grid_spec=pltpu.PrefetchScalarGridSpec(
            num_scalar_prefetch=1,
            grid=(1,),
            in_specs=[pl.BlockSpec(memory_space=pltpu.HBM)],
            out_specs=pl.BlockSpec(memory_space=VMEM),
            scratch_shapes=[pltpu.SemaphoreType.DMA((8 * channels,))],
        ),
        out_shape=jax.ShapeDtypeStruct((channels, beams, phases.shape[2]), jnp.int32),
        compiler_params=pltpu.CompilerParams(vmem_limit_bytes=60 << 20),
        cost_estimate=pl.CostEstimate(flops=0, bytes_accessed=2 << 20, transcendentals=0),
        name="phase_pick",
    )(where, phases)
    received = lax.ppermute(theirs, "quad", swap)

    sent = filter_bank(where, voltages, filter_taps, n)
    spectra = sent[0].shape[0] * LANES

    own = []
    for k in range(n):
        route = [(i, partner(i, size, k, 1)) for i in range(n)]
        own.append(lax.ppermute(sent[k], "chan", route) if k else sent[k])

    pairs = {0: [], 1: []}
    far = []
    for g in range(groups):
        last = g == groups - 1
        blocks = own[g * size : (g + 1) * size]
        got = own_group(geom, where, g, blocks, pairs[g // 2], channels, spectra, not last)
        pairs[g // 2] = got[:2]
        if not last:
            far.append(lax.ppermute(got[2], "quad", swap))
    raw = []
    for k in range((groups - 1) * size, n):
        raw.append(lax.ppermute(own[k], "quad", swap))

    own_gains = gains(where, phases, beams, True)
    far_gains = gains(where, received, beams, False)

    total = n * dishes
    vis_shape = jax.ShapeDtypeStruct((channels, 2, total, n_quad * total), f32)
    q_shape = jax.ShapeDtypeStruct((channels, 2 * beams, 2 * spectra), f32)
    p_shape = jax.ShapeDtypeStruct((channels, beams, spectra), f32)
    half = jax.ShapeDtypeStruct((channels, 2 * LANES, 2 * spectra), bf16)
    near, away = pairs[0], pairs[1]
    wide, narrow = (2 * LANES, 2 * LANES), (2 * LANES, LANES)
    unit = channels * 6 * 2 * (2 * LANES) * (2 * LANES) * 2 * spectra
    late = [VMEM((channels, LANES, 2 * spectra), bf16)] * 2

    vis, q, far_hi, far_lo = products(
        functools.partial(first_kernel, geom), where,
        [*near, far[0], far[1], *own_gains, *far_gains],
        [vis_shape, q_shape, half, half], {}, 4 * channels, wide, [], 4 * unit,
    )
    vis, q = products(
        functools.partial(second_kernel, geom), where,
        [*near, *away, far_hi, far_lo, *own_gains, q, vis],
        [vis_shape, q_shape], {8: 1, 9: 0}, 8 * channels, wide, [], 5 * unit,
    )
    vis, q = products(
        functools.partial(late_kernel, geom, 2, False), where,
        [far[2], *near, *away, *far_gains, q, vis],
        [vis_shape, q_shape], {7: 1, 8: 0}, 4 * channels, narrow, late, 2 * unit,
    )
    vis, power = products(
        functools.partial(late_kernel, geom, 3, True), where,
        [*raw, *near, *away, *far_gains, q, vis],
        [vis_shape, p_shape], {size + 7: 0}, 4 * channels, narrow, late, 2 * unit,
    )
    return vis, power


def solution(mesh):
    n, n_quad = mesh.shape["chan"], mesh.shape["quad"]
    assert n_quad == 2 and n & (n - 1) == 0
    return jax.shard_map(
        functools.partial(per_device, n, n_quad),
        mesh=mesh,
        in_specs=(P("quad", "chan", None, None, None), P(), P("chan", None, "quad")),
        out_specs=(P("chan", None, "quad", None), P("chan", "quad", None)),
        check_vma=False,
    )
```

```python
import functools
import math

import jax
import jax.numpy as jnp
import numpy as np
from jax import lax
from jax.experimental import pallas as pl
from jax.experimental.pallas import tpu as pltpu
from jax.sharding import PartitionSpec as P


PHASE_LEVELS = 256
LANES = 128

f32 = jnp.float32
bf16 = jnp.bfloat16
VMEM = pltpu.VMEM
NT = (((1,), (1,)), ((), ()))
NN = (((1,), (0,)), ((), ()))


def split(x):
    hi = x.astype(bf16)
    return hi, (x - hi.astype(f32)).astype(bf16)


def dot3(a, b, dims):
    mm = functools.partial(lax.dot_general, dimension_numbers=dims, preferred_element_type=f32)
    return mm(a[0], b[0]) + (mm(a[0], b[1]) + mm(a[1], b[0]))


SHIFTS = (0, 1, 3, 2)


def partner(me, size, k, sign):
    z, low = me // size, me % size
    at = ((z ^ (z >> 1)) + 4 + sign * SHIFTS[k // size]) % 4
    return (at ^ (at >> 1)) * size + (low ^ (k % size))


def twiddle_table(fine, per_section):
    n = np.arange(LANES) % fine
    ch = np.arange(fine)
    angle = 2.0 * math.pi * (np.outer(ch, n) % fine) / fine
    cos, sin = np.cos(angle), np.sin(angle)
    table = np.stack([np.stack([cos, -sin], 1), np.stack([sin, cos], 1)], 0)
    table = table.reshape(2, fine // per_section, per_section * 2, LANES)
    return np.ascontiguousarray(table.transpose(1, 0, 2, 3)).astype(np.float32)


def filter_kernel(geom, where, x_ref, table_ref, taps_ref, *rest):
    dishes, coarse, sections, rows4, u_count, j_count, spec_rows, row_count, n = geom
    outs, (coef, coef_hi, coef_lo) = rest[:-3], rest[-3:]
    me = where[0]
    size = n // 4
    chunk = n if coarse == 1 else size
    half = chunk * rows4
    fine = LANES // u_count
    phase = lax.broadcasted_iota(jnp.int32, (1, LANES), 1) // fine
    for k in range(n):
        top, kc = k // chunk * u_count * half, k % chunk
        for i in range(2):
            base = table_ref[partner(me, size, k, 1) % sections, i]
            for u in range(u_count):
                row = top + u * half + kc * rows4
                coef[row : row + rows4, i * LANES : (i + 1) * LANES] = jnp.where(phase == u, base, 0.0)
    coef_hi[...], coef_lo[...] = split(coef[...])

    taps = [taps_ref[t : t + 1, :] for t in range(2 * u_count)]
    weights = []
    for m in range(u_count):
        inside = phase >= m
        first, second = taps[m], taps[u_count + m]
        weights.append(
            (jnp.where(inside, first, 0.0), jnp.where(inside, second, first), jnp.where(inside, 0.0, second))
        )

    def filtered(start):
        rows = [x_ref[pl.ds(start + 2 * j, spec_rows, stride=2), :] for j in range(j_count)]
        total = rows[0] * weights[0][0] + rows[1] * weights[0][1]
        for m in range(1, u_count):
            part = rows[0] * weights[m][0] + rows[1] * weights[m][1] + rows[2] * weights[m][2]
            total = total + pltpu.roll(part, LANES - m * fine, 1)
        return total

    group = u_count
    lane = lax.broadcasted_iota(jnp.int32, (8, LANES), 1)
    sub = lax.broadcasted_iota(jnp.int32, (8, LANES), 0)
    low_lane, low_sub = lane < spec_rows, sub < 4
    for kb in range(n // chunk):
        band = partner(me, size, kb * chunk, 1) // sections if coarse > 1 else 0
        mine = slice(kb * u_count * half, (kb + 1) * u_count * half)

        def step(dg, carry):
            pieces = []
            for d in range(group):
                start = ((dg * group + d) * coarse + band) * row_count * 2
                pieces.append(jnp.concatenate([filtered(start + i) for i in range(2)], axis=1))
            x = split(jnp.concatenate(pieces, axis=0))
            out = dot3((coef_hi[mine, :], coef_lo[mine, :]), x, NT)
            per_tile = 8 // rows4
            for g in range(half // 8):
                for u1 in range(2):
                    tiles = []
                    for d1 in range(2):
                        a0, a1 = (
                            out[
                                (u1 * 2 + u0) * half + g * 8 : (u1 * 2 + u0) * half + g * 8 + 8,
                                d1 * LANES : (d1 + 1) * LANES,
                            ]
                            for u0 in range(2)
                        )
                        tiles.append(jnp.where(low_lane, a0, pltpu.roll(a1, spec_rows, 1)))
                        tiles.append(jnp.where(low_lane, pltpu.roll(a0, spec_rows, 1), a1))
                    for t in range(0, group, per_tile):
                        at = pl.multiple_of((dg * group + t) * rows4, 8)
                        for kk in range(per_tile):
                            k = kb * chunk + per_tile * g + kk
                            if per_tile == 2:
                                b0, b1 = tiles[t], tiles[t + 1]
                                if kk == 0:
                                    tile = jnp.where(low_sub, b0, pltpu.roll(b1, 4, 0))
                                else:
                                    tile = jnp.where(low_sub, pltpu.roll(b0, 4, 0), b1)
                            else:
                                tile = jnp.concatenate(
                                    [b[kk * rows4 : (kk + 1) * rows4] for b in tiles[t : t + per_tile]], axis=0
                                )
                            outs[k][u1, pl.ds(at, 8), :] = tile
            return carry

        lax.fori_loop(0, dishes // group, step, 0, unroll=2)


def rows_kernel(samples, x_ref, out_ref):
    full, tail = samples // LANES, samples % LANES

    def step(d, carry):
        for r in range(full):
            out_ref[d, :, r] = x_ref[0, d, :, :, r * LANES : (r + 1) * LANES]
        if tail:
            out_ref[d, :, full] = jnp.zeros(out_ref.shape[1:2] + out_ref.shape[3:], f32)
            out_ref[d, :, full, :, :tail] = x_ref[0, d, :, :, full * LANES :]
        return carry

    lax.fori_loop(0, x_ref.shape[1], step, 0)


def filter_bank(where, voltages, filter_taps, n):
    _, dishes, coarse, parts, samples = voltages.shape
    taps, fine = filter_taps.shape
    spectra = samples // fine - taps + 1
    per_section = coarse * fine // n
    sections = fine // per_section
    u_count = LANES // fine
    j_count = -(-(u_count - 1 + taps) * fine // LANES)
    spec_rows = spectra // u_count
    row_count = spec_rows + j_count - 1
    rows4 = per_section * 2
    assert u_count == 4 and taps == 8 and j_count == 3 and spec_rows == 64 and rows4 in (2, 4) and dishes % 4 == 0
    x = pl.pallas_call(
        functools.partial(rows_kernel, samples),
        in_specs=[pl.BlockSpec(memory_space=VMEM)],
        out_specs=pl.BlockSpec(memory_space=VMEM),
        out_shape=jax.ShapeDtypeStruct((dishes, coarse, row_count, parts, LANES), f32),
        compiler_params=pltpu.CompilerParams(vmem_limit_bytes=1 << 20),
        cost_estimate=pl.CostEstimate(flops=0, bytes_accessed=4 << 20, transcendentals=0),
        name="rows",
    )(voltages)
    x = x.reshape(dishes * coarse * row_count * parts, LANES)
    taps_rows = jnp.tile(filter_taps, (1, u_count))
    geom = (dishes, coarse, sections, rows4, u_count, j_count, spec_rows, row_count, n)
    width = 2 * LANES
    rows = u_count * n * rows4
    block = jax.ShapeDtypeStruct((spectra // LANES, dishes * rows4, LANES), f32)
    return pl.pallas_call(
        functools.partial(filter_kernel, geom),
        grid_spec=pltpu.PrefetchScalarGridSpec(
            num_scalar_prefetch=1,
            grid=(1,),
            in_specs=[pl.BlockSpec(memory_space=VMEM)] * 3,
            out_specs=[pl.BlockSpec(memory_space=VMEM)] * n,
            scratch_shapes=[VMEM((rows, width), f32), VMEM((rows, width), bf16), VMEM((rows, width), bf16)],
        ),
        out_shape=[block] * n,
        compiler_params=pltpu.CompilerParams(vmem_limit_bytes=12 << 20),
        cost_estimate=pl.CostEstimate(
            flops=6 * rows * width * dishes * spec_rows, bytes_accessed=5 << 20, transcendentals=0
        ),
        name="filter_bank",
    )(where, x, jnp.asarray(twiddle_table(fine, per_section)), taps_rows)


def gain_kernel(where, *refs):
    *pieces, hi_ref, lo_ref = refs
    beams = hi_ref.shape[1] // 2
    row = 0
    for piece in pieces:
        count = piece.shape[1]
        level = piece[0]
        quarter = PHASE_LEVELS // 4
        turn = (level + quarter // 2) // quarter
        x = (level - turn * quarter).astype(f32) * (2.0 * math.pi / PHASE_LEVELS)
        x2 = x * x
        sin = x + x * x2 * (-1.0 / 6 + x2 * (1.0 / 120 + x2 * (-1.0 / 5040 + x2 * (1.0 / 362880))))
        cos = 1.0 + x2 * (-0.5 + x2 * (1.0 / 24 + x2 * (-1.0 / 720 + x2 * (1.0 / 40320 - x2 * (1.0 / 3628800)))))
        odd = (turn & 1) == 1
        c = jnp.where(odd, sin, cos)
        s = jnp.where(odd, cos, sin)
        c = jnp.where(((turn + 1) & 2) == 2, -c, c)
        s = jnp.where((turn & 2) == 2, -s, s)
        hi_ref[0, row : row + count], lo_ref[0, row : row + count] = split(c)
        hi_ref[0, beams + row : beams + row + count], lo_ref[0, beams + row : beams + row + count] = split(s)
        row += count


def gains(where, pieces, beams, local):
    channels, _, dishes = pieces[0].shape
    out = jax.ShapeDtypeStruct((channels, 2 * beams, dishes), bf16)
    whole = pl.BlockSpec((1, 2 * beams, dishes), lambda p, w: (p, 0, 0))
    return pl.pallas_call(
        gain_kernel,
        grid_spec=pltpu.PrefetchScalarGridSpec(
            num_scalar_prefetch=1,
            grid=(channels,),
            in_specs=[
                pl.BlockSpec((1, beams if local else x.shape[1], dishes), lambda p, w: (p, w[1] if local else 0, 0))
                for x in pieces
            ],
            out_specs=[whole, whole],
        ),
        out_shape=[out, out],
        compiler_params=pltpu.CompilerParams(vmem_limit_bytes=(48 if local else 16) << 20),
        cost_estimate=pl.CostEstimate(
            flops=40 * channels * beams * dishes, bytes_accessed=12 * channels * beams * dishes, transcendentals=0
        ),
    )(where, *pieces)


def put(hi, lo, p, at, rows, col, value):
    h, l = split(value)
    hi[p, pl.ds(at, rows), col : col + value.shape[1]] = h
    lo[p, pl.ds(at, rows), col : col + value.shape[1]] = l


def unpack(blocks, first, me, base, dishes, hi, lo, full):
    channels, _, width = hi.shape
    spectra = width // 2
    count = len(blocks)
    pair = 1 if dishes % 16 == 0 else 16 // dishes
    assert pair <= 2
    rows = pair * dishes
    flip = (me % 2) == 1
    for b in range(0, count, pair):
        place = ((me ^ (first + b)) % count) // pair * rows
        for p in range(channels):
            for part in range(2):
                for u in range(spectra // LANES):
                    got = [
                        block[u, pl.ds(p * 2 + part, dishes, stride=channels * 2), :] for block in blocks[b : b + pair]
                    ]
                    if pair == 2:
                        got = [jnp.where(flip, got[1], got[0]), jnp.where(flip, got[0], got[1])]
                    value = jnp.concatenate(got, axis=0)
                    col = part * spectra + u * LANES
                    put(hi, lo, p, pl.multiple_of(base + place, rows), rows, col, value)
                    if full is not None:
                        full[p, pl.ds(pl.multiple_of(place, rows), rows), col : col + LANES] = value


def own_group_kernel(geom, group, *refs):
    _, dishes = geom
    size = LANES // dishes
    blocks = refs[:size]
    outs = refs[size:] if group % 2 == 0 else refs[size + 2 :]
    hi, lo = outs[:2]
    full = outs[2] if len(outs) > 2 else None
    me = lax.axis_index("chan")
    base = group % 2 * LANES
    unpack(blocks, group * size, me, base, dishes, hi, lo, full)


def own_group(geom, group, blocks, pair, channels, spectra, send):
    half = jax.ShapeDtypeStruct((channels, 2 * LANES, 2 * spectra), bf16)
    full = jax.ShapeDtypeStruct((channels, LANES, 2 * spectra), f32)
    whole = pl.BlockSpec(memory_space=VMEM)
    out = [half, half] + ([full] if send else [])
    at = len(blocks)
    return pl.pallas_call(
        functools.partial(own_group_kernel, geom, group),
        in_specs=[whole] * (len(blocks) + len(pair)),
        out_specs=[whole] * len(out),
        out_shape=out,
        input_output_aliases={at: 0, at + 1: 1} if pair else {},
        compiler_params=pltpu.CompilerParams(vmem_limit_bytes=2 << 20),
        cost_estimate=pl.CostEstimate(flops=1 << 20, bytes_accessed=2 << 20, transcendentals=0),
    )(*blocks, *pair)


def turned(x):
    half = x.shape[1] // 2
    return jnp.concatenate([-x[:, half:], x[:, :half]], axis=1)


def beam_terms(g_hi, g_lo, p, ats, x):
    hi, lo = ([g[p, :, pl.ds(pl.multiple_of(at, LANES), LANES)] for at in ats] for g in (g_hi, g_lo))
    left = jnp.concatenate(hi + hi + lo, axis=1)
    right = jnp.concatenate([x[0], x[1], x[0]], axis=0)
    return lax.dot_general(left, right, NN, preferred_element_type=f32)


class Writer:
    def __init__(self, vis, stage, sems, scale):
        self.vis, self.stage, self.sems, self.scale = vis, stage, sems, scale
        self.slots, self.copies = 0, []

    def put(self, p, v, rows, cols, value):
        slot = self.slots
        self.slots += 1
        self.stage[slot] = value * self.scale
        for i, row in enumerate(rows):
            for j, col in enumerate(cols):
                source = self.stage.at[slot, i * LANES : (i + 1) * LANES, j * LANES : (j + 1) * LANES]
                target = self.vis.at[
                    p, v, pl.ds(pl.multiple_of(row, LANES), LANES), pl.ds(pl.multiple_of(col, LANES), LANES)
                ]
                copy = pltpu.make_async_copy(source, target, self.sems.at[len(self.copies)])
                copy.start()
                self.copies.append(copy)

    def wide(self, p, rows, cols, left, right):
        self.put(p, 0, rows, cols, dot3(left, right, NT))
        self.put(p, 1, rows, cols, dot3(left, tuple(turned(r) for r in right), NT))

    def narrow(self, p, rows, cols, left, right):
        both = dot3(left, tuple(jnp.concatenate([r, turned(r)], axis=0) for r in right), NT)
        width = right[0].shape[0]
        self.put(p, 0, rows, cols, both[:, :width])
        self.put(p, 1, rows, cols, both[:, width:])

    def finish(self):
        for copy in self.copies:
            copy.wait()


def places(geom):
    n, dishes = geom
    size = LANES // dishes
    me, quad = lax.axis_index("chan"), lax.axis_index("quad")
    at = [partner(me, size, g * size, -1) // size * LANES for g in range(4)]
    total = n * dishes
    return at, quad * total, (1 - quad) * total


def first_kernel(geom, *refs):
    own_hi, own_lo, far0, far1, gho, glo, ghf, glf, vis, q_ref, far_hi, far_lo, stage, sems = refs
    channels, _, width = own_hi.shape
    at, here, there = places(geom)
    near = at[:2]
    out = Writer(vis, stage, sems, 2.0 / width)
    for p in range(channels):
        for g, far in enumerate((far0, far1)):
            put(far_hi, far_lo, p, g * LANES, LANES, 0, far[p])
        mine, theirs = (own_hi[p], own_lo[p]), (far_hi[p], far_lo[p])
        out.wide(p, near, [here + a for a in near], mine, mine)
        out.wide(p, near, [there + a for a in near], mine, theirs)
        q_ref[p] = beam_terms(gho, glo, p, near, mine) + beam_terms(ghf, glf, p, near, theirs)
    out.finish()


def second_kernel(geom, *refs):
    near_hi, near_lo, own_hi, own_lo, far_hi, far_lo, gho, glo, q_in, _, vis, q_ref, stage, sems = refs
    channels, _, width = own_hi.shape
    at, here, there = places(geom)
    near, away = at[:2], at[2:]
    out = Writer(vis, stage, sems, 2.0 / width)
    for p in range(channels):
        first, mine, theirs = (near_hi[p], near_lo[p]), (own_hi[p], own_lo[p]), (far_hi[p], far_lo[p])
        out.wide(p, away, [here + a for a in away], mine, mine)
        out.wide(p, away, [here + a for a in near], mine, first)
        out.wide(p, near, [here + a for a in away], first, mine)
        out.wide(p, away, [there + a for a in near], mine, theirs)
        q_ref[p] = q_in[p] + beam_terms(gho, glo, p, away, mine)
    out.finish()


def late_kernel(geom, group, raw, *refs):
    n, dishes = geom
    size = LANES // dishes
    got, refs = refs[: size if raw else 1], refs[size if raw else 1 :]
    near_hi, near_lo, own_hi, own_lo, ghf, glf, q_in, _, vis, q_ref, stage, sems = refs[:12]
    hi, lo, *more = refs[12:]
    channels, _, width = own_hi.shape
    at, _, there = places(geom)
    col = there + at[group]
    if raw:
        unpack(got, group * size, lax.axis_index("chan"), 0, dishes, hi, lo, None)
    out = Writer(vis, stage, sems, 2.0 / width)
    copies = []
    for p in range(channels):
        if not raw:
            put(hi, lo, p, 0, LANES, 0, got[0][p])
        q = q_in[p] + beam_terms(ghf, glf, p, [at[group]], (hi[p], lo[p]))
        if not raw:
            q_ref[p] = q
            continue
        held, held_sems = more
        beams, spectra = q.shape[0] // 2, q.shape[1] // 2
        re = q[:beams, :spectra] + q[beams:, spectra:]
        im = q[:beams, spectra:] - q[beams:, :spectra]
        power = (re * re + im * im) * (1.0 / (2 * n * dishes))
        u_count = spectra // 64
        got_at = lax.broadcasted_iota(jnp.int32, (spectra, spectra), 0)
        want_at = lax.broadcasted_iota(jnp.int32, (spectra, spectra), 1)
        pick = ((got_at % 64) * u_count + got_at // 64 == want_at).astype(bf16)
        ordered = jnp.zeros_like(power)
        for _ in range(3):
            piece = power.astype(bf16)
            ordered += lax.dot_general(piece, pick, NN, preferred_element_type=f32)
            power = power - piece.astype(f32)
        held[p] = ordered
        copy = pltpu.make_async_copy(held.at[p], q_ref.at[p], held_sems.at[p])
        copy.start()
        copies.append(copy)
    for p in range(channels):
        x = (hi[p], lo[p])
        out.narrow(p, at[:2], [col], (near_hi[p], near_lo[p]), x)
        out.narrow(p, at[2:], [col], (own_hi[p], own_lo[p]), x)
    for copy in copies:
        copy.wait()
    out.finish()


def products(kernel, ins, outs, aliases, slots, block, more, flops, last=False):
    whole, where_it_is = pl.BlockSpec(memory_space=VMEM), pl.BlockSpec(memory_space=pl.ANY)
    vis_shape = outs[0].shape
    return pl.pallas_call(
        kernel,
        in_specs=[where_it_is if x.shape == vis_shape else whole for x in ins],
        out_specs=[where_it_is] + [where_it_is if x.dtype == f32 and last else whole for x in outs[1:]],
        scratch_shapes=[VMEM((slots,) + block, f32), pltpu.SemaphoreType.DMA((4 * slots,))] + more,
        out_shape=outs,
        input_output_aliases=aliases,
        compiler_params=pltpu.CompilerParams(vmem_limit_bytes=16 << 20),
        cost_estimate=pl.CostEstimate(flops=flops, bytes_accessed=4 << 20, transcendentals=0),
    )(*ins)


def phase_kernel(beams, first, phases, out, sems):
    channels, count, _ = out.shape
    pieces = sems.shape[0] // channels
    rows = count // pieces
    at = (1 - lax.axis_index("quad")) * beams + first
    copies = []
    for p in range(channels):
        for i in range(pieces):
            copies.append(
                pltpu.make_async_copy(
                    phases.at[p, pl.ds(pl.multiple_of(at + i * rows, rows), rows), :],
                    out.at[p, i * rows : (i + 1) * rows, :],
                    sems.at[p * pieces + i],
                )
            )
    for copy in copies:
        copy.start()
    for copy in copies:
        copy.wait()


def phase_piece(phases, beams, first, count):
    channels, _, dishes = phases.shape
    pieces = count // 32
    return pl.pallas_call(
        functools.partial(phase_kernel, beams, first),
        in_specs=[pl.BlockSpec(memory_space=pltpu.HBM)],
        out_specs=pl.BlockSpec(memory_space=VMEM),
        scratch_shapes=[pltpu.SemaphoreType.DMA((pieces * channels,))],
        out_shape=jax.ShapeDtypeStruct((channels, count, dishes), jnp.int32),
        compiler_params=pltpu.CompilerParams(vmem_limit_bytes=60 << 20),
        cost_estimate=pl.CostEstimate(flops=0, bytes_accessed=2 << 20, transcendentals=0),
    )(phases)


def per_device(n, n_quad, voltages, filter_taps, phases):
    return whole_step(n, n_quad, voltages, filter_taps, phases)


def whole_step(n, n_quad, voltages, filter_taps, phases):
    dishes = voltages.shape[1]
    channels, beams_all, _ = phases.shape
    beams = beams_all // n_quad
    size = LANES // dishes
    groups = n // size
    assert groups == 4
    geom = (n, dishes)
    me = lax.axis_index("chan").astype(jnp.int32)
    quad = lax.axis_index("quad").astype(jnp.int32)
    where = jnp.stack([me, quad])
    swap = [(0, 1), (1, 0)]

    received = []
    for first, count in ((0, beams),):
        piece = phase_piece(phases, beams, first, count)
        received.append(lax.ppermute(piece, "quad", swap))

    sent = filter_bank(where, voltages, filter_taps, n)
    spectra = sent[0].shape[0] * LANES

    own = []
    for k in range(n):
        route = [(i, partner(i, size, k, 1)) for i in range(n)]
        own.append(lax.ppermute(sent[k], "chan", route) if k else sent[k])

    pairs = {0: [], 1: []}
    far = []
    for g in range(groups):
        last = g == groups - 1
        blocks = own[g * size : (g + 1) * size]
        got = own_group(geom, g, blocks, pairs[g // 2], channels, spectra, not last)
        pairs[g // 2] = got[:2]
        if not last:
            far.append(lax.ppermute(got[2], "quad", swap))
    raw = []
    for k in range((groups - 1) * size, n):
        raw.append(lax.ppermute(own[k], "quad", swap))

    own_gains = gains(where, [phases], beams, True)
    far_gains = gains(where, received, beams, False)

    total = n * dishes
    vis_shape = jax.ShapeDtypeStruct((channels, 2, total, n_quad * total), f32)
    q_shape = jax.ShapeDtypeStruct((channels, 2 * beams, 2 * spectra), f32)
    p_shape = jax.ShapeDtypeStruct((channels, beams, spectra), f32)
    half = jax.ShapeDtypeStruct((channels, 2 * LANES, 2 * spectra), bf16)
    near, away = pairs[0], pairs[1]
    wide, narrow = (2 * LANES, 2 * LANES), (2 * LANES, LANES)
    unit = channels * 6 * 2 * (2 * LANES) * (2 * LANES) * 2 * spectra
    late = [VMEM((channels, LANES, 2 * spectra), bf16)] * 2
    power = [VMEM((channels, beams, spectra), f32), pltpu.SemaphoreType.DMA((channels,))]

    vis, q, far_hi, far_lo = products(
        functools.partial(first_kernel, geom),
        [*near, far[0], far[1], *own_gains, *far_gains],
        [vis_shape, q_shape, half, half], {}, 4 * channels, wide, [], 4 * unit,
    )
    vis, q = products(
        functools.partial(second_kernel, geom),
        [*near, *away, far_hi, far_lo, *own_gains, q, vis],
        [vis_shape, q_shape], {8: 1, 9: 0}, 8 * channels, wide, [], 5 * unit,
    )
    vis, q = products(
        functools.partial(late_kernel, geom, 2, False),
        [far[2], *near, *away, *far_gains, q, vis],
        [vis_shape, q_shape], {7: 1, 8: 0}, 4 * channels, narrow, late, 2 * unit,
    )
    vis, power = products(
        functools.partial(late_kernel, geom, 3, True),
        [*raw, *near, *away, *far_gains, q, vis],
        [vis_shape, p_shape], {size + 7: 0}, 4 * channels, narrow, late + power, 2 * unit, True,
    )
    return vis, power


def solution(mesh):
    n, n_quad = mesh.shape["chan"], mesh.shape["quad"]
    assert n_quad == 2 and n & (n - 1) == 0
    return jax.shard_map(
        functools.partial(per_device, n, n_quad),
        mesh=mesh,
        in_specs=(P("quad", "chan", None, None, None), P(), P("chan", None, "quad")),
        out_specs=(P("chan", None, "quad", None), P("chan", "quad", None)),
        check_vma=False,
    )
```

```python
import functools
import math

import jax
import jax.numpy as jnp
import numpy as np
from jax import lax
from jax.experimental import pallas as pl
from jax.experimental.pallas import tpu as pltpu
from jax.sharding import PartitionSpec as P


PHASE_LEVELS = 256
LANES = 128

f32 = jnp.float32
bf16 = jnp.bfloat16
VMEM = pltpu.VMEM
NT = (((1,), (1,)), ((), ()))
NN = (((1,), (0,)), ((), ()))


def split(x):
    hi = x.astype(bf16)
    return hi, (x - hi.astype(f32)).astype(bf16)


def dot3(a, b, dims):
    mm = functools.partial(lax.dot_general, dimension_numbers=dims, preferred_element_type=f32)
    return mm(a[0], b[0]) + (mm(a[0], b[1]) + mm(a[1], b[0]))


SHIFTS = (0, 1, 3, 2)


def partner(me, size, k, sign):
    z, low = me // size, me % size
    at = ((z ^ (z >> 1)) + 4 + sign * SHIFTS[k // size]) % 4
    return (at ^ (at >> 1)) * size + (low ^ (k % size))


def twiddle_table(fine, per_section):
    n = np.arange(LANES) % fine
    ch = np.arange(fine)
    angle = 2.0 * math.pi * (np.outer(ch, n) % fine) / fine
    cos, sin = np.cos(angle), np.sin(angle)
    table = np.stack([np.stack([cos, -sin], 1), np.stack([sin, cos], 1)], 0)
    table = table.reshape(2, fine // per_section, per_section * 2, LANES)
    return np.ascontiguousarray(table.transpose(1, 0, 2, 3)).astype(np.float32)


def filter_kernel(geom, where, x_ref, table_ref, taps_ref, *rest):
    dishes, coarse, sections, rows4, u_count, j_count, spec_rows, row_count, n = geom
    outs, (coef, coef_hi, coef_lo) = rest[:-3], rest[-3:]
    me = where[0]
    size = n // 4
    chunk = n if coarse == 1 else size
    half = chunk * rows4
    fine = LANES // u_count
    phase = lax.broadcasted_iota(jnp.int32, (1, LANES), 1) // fine
    for k in range(n):
        top, kc = k // chunk * u_count * half, k % chunk
        for i in range(2):
            base = table_ref[partner(me, size, k, 1) % sections, i]
            for u in range(u_count):
                row = top + u * half + kc * rows4
                coef[row : row + rows4, i * LANES : (i + 1) * LANES] = jnp.where(phase == u, base, 0.0)
    coef_hi[...], coef_lo[...] = split(coef[...])

    taps = [taps_ref[t : t + 1, :] for t in range(2 * u_count)]
    weights = []
    for m in range(u_count):
        inside = phase >= m
        first, second = taps[m], taps[u_count + m]
        weights.append(
            (jnp.where(inside, first, 0.0), jnp.where(inside, second, first), jnp.where(inside, 0.0, second))
        )

    def filtered(start):
        rows = [x_ref[pl.ds(start + 2 * j, spec_rows, stride=2), :] for j in range(j_count)]
        total = rows[0] * weights[0][0] + rows[1] * weights[0][1]
        for m in range(1, u_count):
            part = rows[0] * weights[m][0] + rows[1] * weights[m][1] + rows[2] * weights[m][2]
            total = total + pltpu.roll(part, LANES - m * fine, 1)
        return total

    group = u_count
    lane = lax.broadcasted_iota(jnp.int32, (8, LANES), 1)
    sub = lax.broadcasted_iota(jnp.int32, (8, LANES), 0)
    low_lane, low_sub = lane < spec_rows, sub < 4
    for kb in range(n // chunk):
        band = partner(me, size, kb * chunk, 1) // sections if coarse > 1 else 0
        mine = slice(kb * u_count * half, (kb + 1) * u_count * half)

        def step(dg, carry):
            pieces = []
            for d in range(group):
                start = ((dg * group + d) * coarse + band) * row_count * 2
                pieces.append(jnp.concatenate([filtered(start + i) for i in range(2)], axis=1))
            x = split(jnp.concatenate(pieces, axis=0))
            out = dot3((coef_hi[mine, :], coef_lo[mine, :]), x, NT)
            per_tile = 8 // rows4
            for g in range(half // 8):
                for u1 in range(2):
                    tiles = []
                    for d1 in range(2):
                        a0, a1 = (
                            out[
                                (u1 * 2 + u0) * half + g * 8 : (u1 * 2 + u0) * half + g * 8 + 8,
                                d1 * LANES : (d1 + 1) * LANES,
                            ]
                            for u0 in range(2)
                        )
                        tiles.append(jnp.where(low_lane, a0, pltpu.roll(a1, spec_rows, 1)))
                        tiles.append(jnp.where(low_lane, pltpu.roll(a0, spec_rows, 1), a1))
                    for t in range(0, group, per_tile):
                        at = pl.multiple_of((dg * group + t) * rows4, 8)
                        for kk in range(per_tile):
                            k = kb * chunk + per_tile * g + kk
                            if per_tile == 2:
                                b0, b1 = tiles[t], tiles[t + 1]
                                if kk == 0:
                                    tile = jnp.where(low_sub, b0, pltpu.roll(b1, 4, 0))
                                else:
                                    tile = jnp.where(low_sub, pltpu.roll(b0, 4, 0), b1)
                            else:
                                tile = jnp.concatenate(
                                    [b[kk * rows4 : (kk + 1) * rows4] for b in tiles[t : t + per_tile]], axis=0
                                )
                            outs[k][u1, pl.ds(at, 8), :] = tile
            return carry

        lax.fori_loop(0, dishes // group, step, 0, unroll=2)


def rows_kernel(samples, x_ref, out_ref):
    full, tail = samples // LANES, samples % LANES

    def step(d, carry):
        for r in range(full):
            out_ref[d, :, r] = x_ref[0, d, :, :, r * LANES : (r + 1) * LANES]
        if tail:
            out_ref[d, :, full] = jnp.zeros(out_ref.shape[1:2] + out_ref.shape[3:], f32)
            out_ref[d, :, full, :, :tail] = x_ref[0, d, :, :, full * LANES :]
        return carry

    lax.fori_loop(0, x_ref.shape[1], step, 0)


def filter_bank(where, voltages, filter_taps, n):
    _, dishes, coarse, parts, samples = voltages.shape
    taps, fine = filter_taps.shape
    spectra = samples // fine - taps + 1
    per_section = coarse * fine // n
    sections = fine // per_section
    u_count = LANES // fine
    j_count = -(-(u_count - 1 + taps) * fine // LANES)
    spec_rows = spectra // u_count
    row_count = spec_rows + j_count - 1
    rows4 = per_section * 2
    assert u_count == 4 and taps == 8 and j_count == 3 and spec_rows == 64 and rows4 in (2, 4) and dishes % 4 == 0
    x = pl.pallas_call(
        functools.partial(rows_kernel, samples),
        in_specs=[pl.BlockSpec(memory_space=VMEM)],
        out_specs=pl.BlockSpec(memory_space=VMEM),
        out_shape=jax.ShapeDtypeStruct((dishes, coarse, row_count, parts, LANES), f32),
        compiler_params=pltpu.CompilerParams(vmem_limit_bytes=1 << 20),
        cost_estimate=pl.CostEstimate(flops=0, bytes_accessed=4 << 20, transcendentals=0),
        name="rows",
    )(voltages)
    x = x.reshape(dishes * coarse * row_count * parts, LANES)
    taps_rows = jnp.tile(filter_taps, (1, u_count))
    geom = (dishes, coarse, sections, rows4, u_count, j_count, spec_rows, row_count, n)
    width = 2 * LANES
    rows = u_count * n * rows4
    block = jax.ShapeDtypeStruct((spectra // LANES, dishes * rows4, LANES), f32)
    return pl.pallas_call(
        functools.partial(filter_kernel, geom),
        grid_spec=pltpu.PrefetchScalarGridSpec(
            num_scalar_prefetch=1,
            grid=(1,),
            in_specs=[pl.BlockSpec(memory_space=VMEM)] * 3,
            out_specs=[pl.BlockSpec(memory_space=VMEM)] * n,
            scratch_shapes=[VMEM((rows, width), f32), VMEM((rows, width), bf16), VMEM((rows, width), bf16)],
        ),
        out_shape=[block] * n,
        compiler_params=pltpu.CompilerParams(vmem_limit_bytes=12 << 20),
        cost_estimate=pl.CostEstimate(
            flops=6 * rows * width * dishes * spec_rows, bytes_accessed=5 << 20, transcendentals=0
        ),
        name="filter_bank",
    )(where, x, jnp.asarray(twiddle_table(fine, per_section)), taps_rows)


def gain_kernel(where, *refs):
    *pieces, hi_ref, lo_ref = refs
    beams = hi_ref.shape[1] // 2
    row = 0
    for piece in pieces:
        count = piece.shape[1]
        level = piece[0]
        quarter = PHASE_LEVELS // 4
        turn = (level + quarter // 2) // quarter
        x = (level - turn * quarter).astype(f32) * (2.0 * math.pi / PHASE_LEVELS)
        x2 = x * x
        sin = x + x * x2 * (-1.0 / 6 + x2 * (1.0 / 120 + x2 * (-1.0 / 5040 + x2 * (1.0 / 362880))))
        cos = 1.0 + x2 * (-0.5 + x2 * (1.0 / 24 + x2 * (-1.0 / 720 + x2 * (1.0 / 40320 - x2 * (1.0 / 3628800)))))
        odd = (turn & 1) == 1
        c = jnp.where(odd, sin, cos)
        s = jnp.where(odd, cos, sin)
        c = jnp.where(((turn + 1) & 2) == 2, -c, c)
        s = jnp.where((turn & 2) == 2, -s, s)
        hi_ref[0, row : row + count], lo_ref[0, row : row + count] = split(c)
        hi_ref[0, beams + row : beams + row + count], lo_ref[0, beams + row : beams + row + count] = split(s)
        row += count


def gains(where, pieces, beams, local):
    channels, _, dishes = pieces[0].shape
    out = jax.ShapeDtypeStruct((channels, 2 * beams, dishes), bf16)
    whole = pl.BlockSpec((1, 2 * beams, dishes), lambda p, w: (p, 0, 0))
    return pl.pallas_call(
        gain_kernel,
        grid_spec=pltpu.PrefetchScalarGridSpec(
            num_scalar_prefetch=1,
            grid=(channels,),
            in_specs=[
                pl.BlockSpec((1, beams if local else x.shape[1], dishes), lambda p, w: (p, w[1] if local else 0, 0))
                for x in pieces
            ],
            out_specs=[whole, whole],
        ),
        out_shape=[out, out],
        compiler_params=pltpu.CompilerParams(vmem_limit_bytes=(48 if local else 16) << 20),
        cost_estimate=pl.CostEstimate(
            flops=40 * channels * beams * dishes, bytes_accessed=12 * channels * beams * dishes, transcendentals=0
        ),
    )(where, *pieces)


def put(hi, lo, p, at, rows, col, value):
    h, l = split(value)
    hi[p, pl.ds(at, rows), col : col + value.shape[1]] = h
    lo[p, pl.ds(at, rows), col : col + value.shape[1]] = l


def unpack(blocks, first, me, base, dishes, hi, lo, full):
    channels, _, width = hi.shape
    spectra = width // 2
    count = len(blocks)
    pair = 1 if dishes % 16 == 0 else 16 // dishes
    assert pair <= 2
    rows = pair * dishes
    flip = (me % 2) == 1
    for b in range(0, count, pair):
        place = ((me ^ (first + b)) % count) // pair * rows
        for p in range(channels):
            for part in range(2):
                for u in range(spectra // LANES):
                    got = [
                        block[u, pl.ds(p * 2 + part, dishes, stride=channels * 2), :] for block in blocks[b : b + pair]
                    ]
                    if pair == 2:
                        got = [jnp.where(flip, got[1], got[0]), jnp.where(flip, got[0], got[1])]
                    value = jnp.concatenate(got, axis=0)
                    col = part * spectra + u * LANES
                    put(hi, lo, p, pl.multiple_of(base + place, rows), rows, col, value)
                    if full is not None:
                        full[p, pl.ds(pl.multiple_of(place, rows), rows), col : col + LANES] = value


def own_group_kernel(geom, group, *refs):
    _, dishes = geom
    size = LANES // dishes
    blocks = refs[:size]
    outs = refs[size:] if group % 2 == 0 else refs[size + 2 :]
    hi, lo = outs[:2]
    full = outs[2] if len(outs) > 2 else None
    me = lax.axis_index("chan")
    base = group % 2 * LANES
    unpack(blocks, group * size, me, base, dishes, hi, lo, full)


def own_group(geom, group, blocks, pair, channels, spectra, send):
    half = jax.ShapeDtypeStruct((channels, 2 * LANES, 2 * spectra), bf16)
    full = jax.ShapeDtypeStruct((channels, LANES, 2 * spectra), f32)
    whole = pl.BlockSpec(memory_space=VMEM)
    out = [half, half] + ([full] if send else [])
    at = len(blocks)
    return pl.pallas_call(
        functools.partial(own_group_kernel, geom, group),
        in_specs=[whole] * (len(blocks) + len(pair)),
        out_specs=[whole] * len(out),
        out_shape=out,
        input_output_aliases={at: 0, at + 1: 1} if pair else {},
        compiler_params=pltpu.CompilerParams(vmem_limit_bytes=2 << 20),
        cost_estimate=pl.CostEstimate(flops=1 << 20, bytes_accessed=2 << 20, transcendentals=0),
    )(*blocks, *pair)


def turned(x):
    half = x.shape[1] // 2
    return jnp.concatenate([-x[:, half:], x[:, :half]], axis=1)


def beam_terms(g_hi, g_lo, p, ats, x):
    hi, lo = ([g[p, :, pl.ds(pl.multiple_of(at, LANES), LANES)] for at in ats] for g in (g_hi, g_lo))
    left = jnp.concatenate(hi + hi + lo, axis=1)
    right = jnp.concatenate([x[0], x[1], x[0]], axis=0)
    return lax.dot_general(left, right, NN, preferred_element_type=f32)


class Writer:
    def __init__(self, vis, stage, sems, scale):
        self.vis, self.stage, self.sems, self.scale = vis, stage, sems, scale
        self.slots, self.copies = 0, []

    def put(self, p, v, rows, cols, value):
        slot = self.slots
        self.slots += 1
        self.stage[slot] = value * self.scale
        for i, row in enumerate(rows):
            for j, col in enumerate(cols):
                source = self.stage.at[slot, i * LANES : (i + 1) * LANES, j * LANES : (j + 1) * LANES]
                target = self.vis.at[
                    p, v, pl.ds(pl.multiple_of(row, LANES), LANES), pl.ds(pl.multiple_of(col, LANES), LANES)
                ]
                copy = pltpu.make_async_copy(source, target, self.sems.at[len(self.copies)])
                copy.start()
                self.copies.append(copy)

    def wide(self, p, rows, cols, left, right):
        self.put(p, 0, rows, cols, dot3(left, right, NT))
        self.put(p, 1, rows, cols, dot3(left, tuple(turned(r) for r in right), NT))

    def narrow(self, p, rows, cols, left, right):
        both = dot3(left, tuple(jnp.concatenate([r, turned(r)], axis=0) for r in right), NT)
        width = right[0].shape[0]
        self.put(p, 0, rows, cols, both[:, :width])
        self.put(p, 1, rows, cols, both[:, width:])

    def finish(self):
        for copy in self.copies:
            copy.wait()


def places(geom):
    n, dishes = geom
    size = LANES // dishes
    me, quad = lax.axis_index("chan"), lax.axis_index("quad")
    at = [partner(me, size, g * size, -1) // size * LANES for g in range(4)]
    total = n * dishes
    return at, quad * total, (1 - quad) * total


def first_kernel(geom, *refs):
    own_hi, own_lo, far0, far1, gho, glo, ghf, glf, vis, q_ref, far_hi, far_lo, stage, sems = refs
    channels, _, width = own_hi.shape
    at, here, there = places(geom)
    near = at[:2]
    out = Writer(vis, stage, sems, 2.0 / width)
    for p in range(channels):
        for g, far in enumerate((far0, far1)):
            put(far_hi, far_lo, p, g * LANES, LANES, 0, far[p])
        mine, theirs = (own_hi[p], own_lo[p]), (far_hi[p], far_lo[p])
        out.wide(p, near, [here + a for a in near], mine, mine)
        out.wide(p, near, [there + a for a in near], mine, theirs)
        q_ref[p] = beam_terms(gho, glo, p, near, mine) + beam_terms(ghf, glf, p, near, theirs)
    out.finish()


def second_kernel(geom, *refs):
    near_hi, near_lo, own_hi, own_lo, far_hi, far_lo, gho, glo, q_in, _, vis, q_ref, stage, sems = refs
    channels, _, width = own_hi.shape
    at, here, there = places(geom)
    near, away = at[:2], at[2:]
    out = Writer(vis, stage, sems, 2.0 / width)
    for p in range(channels):
        first, mine, theirs = (near_hi[p], near_lo[p]), (own_hi[p], own_lo[p]), (far_hi[p], far_lo[p])
        out.wide(p, away, [here + a for a in away], mine, mine)
        out.wide(p, away, [here + a for a in near], mine, first)
        out.wide(p, near, [here + a for a in away], first, mine)
        out.wide(p, away, [there + a for a in near], mine, theirs)
        q_ref[p] = q_in[p] + beam_terms(gho, glo, p, away, mine)
    out.finish()


def late_kernel(geom, group, raw, *refs):
    n, dishes = geom
    size = LANES // dishes
    got, refs = refs[: size if raw else 1], refs[size if raw else 1 :]
    near_hi, near_lo, own_hi, own_lo, ghf, glf, q_in, _, vis, q_ref, stage, sems = refs[:12]
    hi, lo, *more = refs[12:]
    channels, _, width = own_hi.shape
    at, _, there = places(geom)
    col = there + at[group]
    if raw:
        unpack(got, group * size, lax.axis_index("chan"), 0, dishes, hi, lo, None)
    out = Writer(vis, stage, sems, 2.0 / width)
    copies = []
    for p in range(channels):
        if not raw:
            put(hi, lo, p, 0, LANES, 0, got[0][p])
        q = q_in[p] + beam_terms(ghf, glf, p, [at[group]], (hi[p], lo[p]))
        if not raw:
            q_ref[p] = q
            continue
        held, held_sems = more
        beams, spectra = q.shape[0] // 2, q.shape[1] // 2
        re = q[:beams, :spectra] + q[beams:, spectra:]
        im = q[:beams, spectra:] - q[beams:, :spectra]
        power = (re * re + im * im) * (1.0 / (2 * n * dishes))
        lane = lax.broadcasted_iota(jnp.int32, (beams, LANES), 1)
        for h in range(spectra // LANES):
            at_lane = lane % 2 * 64 + 32 * h + lane // 4
            low, high = (
                jnp.take_along_axis(power[:, i * LANES : (i + 1) * LANES], at_lane, axis=1, mode="promise_in_bounds")
                for i in range(2)
            )
            held[p, :, h * LANES : (h + 1) * LANES] = jnp.where(lane % 4 < 2, low, high)
        copy = pltpu.make_async_copy(held.at[p], q_ref.at[p], held_sems.at[p])
        copy.start()
        copies.append(copy)
    for p in range(channels):
        x = (hi[p], lo[p])
        out.narrow(p, at[:2], [col], (near_hi[p], near_lo[p]), x)
        out.narrow(p, at[2:], [col], (own_hi[p], own_lo[p]), x)
    for copy in copies:
        copy.wait()
    out.finish()


def products(kernel, ins, outs, aliases, slots, block, more, flops, last=False):
    whole, where_it_is = pl.BlockSpec(memory_space=VMEM), pl.BlockSpec(memory_space=pl.ANY)
    vis_shape = outs[0].shape
    return pl.pallas_call(
        kernel,
        in_specs=[where_it_is if x.shape == vis_shape else whole for x in ins],
        out_specs=[where_it_is] + [where_it_is if x.dtype == f32 and last else whole for x in outs[1:]],
        scratch_shapes=[VMEM((slots,) + block, f32), pltpu.SemaphoreType.DMA((4 * slots,))] + more,
        out_shape=outs,
        input_output_aliases=aliases,
        compiler_params=pltpu.CompilerParams(vmem_limit_bytes=16 << 20),
        cost_estimate=pl.CostEstimate(flops=flops, bytes_accessed=4 << 20, transcendentals=0),
    )(*ins)


def phase_kernel(beams, first, phases, out, sems):
    channels, count, _ = out.shape
    pieces = sems.shape[0] // channels
    rows = count // pieces
    at = (1 - lax.axis_index("quad")) * beams + first
    copies = []
    for p in range(channels):
        for i in range(pieces):
            copies.append(
                pltpu.make_async_copy(
                    phases.at[p, pl.ds(pl.multiple_of(at + i * rows, rows), rows), :],
                    out.at[p, i * rows : (i + 1) * rows, :],
                    sems.at[p * pieces + i],
                )
            )
    for copy in copies:
        copy.start()
    for copy in copies:
        copy.wait()


def phase_piece(phases, beams, first, count):
    channels, _, dishes = phases.shape
    pieces = count // 32
    return pl.pallas_call(
        functools.partial(phase_kernel, beams, first),
        in_specs=[pl.BlockSpec(memory_space=pltpu.HBM)],
        out_specs=pl.BlockSpec(memory_space=VMEM),
        scratch_shapes=[pltpu.SemaphoreType.DMA((pieces * channels,))],
        out_shape=jax.ShapeDtypeStruct((channels, count, dishes), jnp.int32),
        compiler_params=pltpu.CompilerParams(vmem_limit_bytes=52 << 20),
        cost_estimate=pl.CostEstimate(flops=0, bytes_accessed=2 << 20, transcendentals=0),
    )(phases)


def per_device(n, n_quad, voltages, filter_taps, phases):
    return whole_step(n, n_quad, voltages, filter_taps, phases)


def whole_step(n, n_quad, voltages, filter_taps, phases):
    dishes = voltages.shape[1]
    channels, beams_all, _ = phases.shape
    beams = beams_all // n_quad
    size = LANES // dishes
    groups = n // size
    assert groups == 4
    geom = (n, dishes)
    me = lax.axis_index("chan").astype(jnp.int32)
    quad = lax.axis_index("quad").astype(jnp.int32)
    where = jnp.stack([me, quad])
    swap = [(0, 1), (1, 0)]

    received = []
    for first, count in ((0, beams),):
        piece = phase_piece(phases, beams, first, count)
        received.append(lax.ppermute(piece, "quad", swap))

    sent = filter_bank(where, voltages, filter_taps, n)
    spectra = sent[0].shape[0] * LANES

    own = []
    for k in range(n):
        route = [(i, partner(i, size, k, 1)) for i in range(n)]
        own.append(lax.ppermute(sent[k], "chan", route) if k else sent[k])

    pairs = {0: [], 1: []}
    far = []
    for g in range(groups):
        last = g == groups - 1
        blocks = own[g * size : (g + 1) * size]
        got = own_group(geom, g, blocks, pairs[g // 2], channels, spectra, not last)
        pairs[g // 2] = got[:2]
        if not last:
            far.append(lax.ppermute(got[2], "quad", swap))
    raw = []
    for k in range((groups - 1) * size, n):
        raw.append(lax.ppermute(own[k], "quad", swap))

    own_gains = gains(where, [phases], beams, True)
    far_gains = gains(where, received, beams, False)

    total = n * dishes
    vis_shape = jax.ShapeDtypeStruct((channels, 2, total, n_quad * total), f32)
    q_shape = jax.ShapeDtypeStruct((channels, 2 * beams, 2 * spectra), f32)
    p_shape = jax.ShapeDtypeStruct((channels, beams, spectra), f32)
    half = jax.ShapeDtypeStruct((channels, 2 * LANES, 2 * spectra), bf16)
    near, away = pairs[0], pairs[1]
    wide, narrow = (2 * LANES, 2 * LANES), (2 * LANES, LANES)
    unit = channels * 6 * 2 * (2 * LANES) * (2 * LANES) * 2 * spectra
    late = [VMEM((channels, LANES, 2 * spectra), bf16)] * 2
    power = [VMEM((channels, beams, spectra), f32), pltpu.SemaphoreType.DMA((channels,))]

    vis, q, far_hi, far_lo = products(
        functools.partial(first_kernel, geom),
        [*near, far[0], far[1], *own_gains, *far_gains],
        [vis_shape, q_shape, half, half], {}, 4 * channels, wide, [], 4 * unit,
    )
    vis, q = products(
        functools.partial(second_kernel, geom),
        [*near, *away, far_hi, far_lo, *own_gains, q, vis],
        [vis_shape, q_shape], {8: 1, 9: 0}, 8 * channels, wide, [], 5 * unit,
    )
    vis, q = products(
        functools.partial(late_kernel, geom, 2, False),
        [far[2], *near, *away, *far_gains, q, vis],
        [vis_shape, q_shape], {7: 1, 8: 0}, 4 * channels, narrow, late, 2 * unit,
    )
    vis, power = products(
        functools.partial(late_kernel, geom, 3, True),
        [*raw, *near, *away, *far_gains, q, vis],
        [vis_shape, p_shape], {size + 7: 0}, 4 * channels, narrow, late + power, 2 * unit, True,
    )
    return vis, power


def solution(mesh):
    n, n_quad = mesh.shape["chan"], mesh.shape["quad"]
    assert n_quad == 2 and n & (n - 1) == 0
    return jax.shard_map(
        functools.partial(per_device, n, n_quad),
        mesh=mesh,
        in_specs=(P("quad", "chan", None, None, None), P(), P("chan", None, "quad")),
        out_specs=(P("chan", None, "quad", None), P("chan", "quad", None)),
        check_vma=False,
    )
```

```python
import functools
import math

import jax
import jax.numpy as jnp
import numpy as np
from jax import lax
from jax.experimental import pallas as pl
from jax.experimental.pallas import tpu as pltpu
from jax.sharding import PartitionSpec as P


PHASE_LEVELS = 256
LANES = 128

f32 = jnp.float32
bf16 = jnp.bfloat16
VMEM = pltpu.VMEM
NT = (((1,), (1,)), ((), ()))
NN = (((1,), (0,)), ((), ()))


def split(x):
    hi = x.astype(bf16)
    return hi, (x - hi.astype(f32)).astype(bf16)


def dot3(a, b, dims):
    mm = functools.partial(lax.dot_general, dimension_numbers=dims, preferred_element_type=f32)
    return mm(a[0], b[0]) + (mm(a[0], b[1]) + mm(a[1], b[0]))


SHIFTS = (0, 1, 3, 2)


def partner(me, size, k, sign):
    z, low = me // size, me % size
    at = ((z ^ (z >> 1)) + 4 + sign * SHIFTS[k // size]) % 4
    return (at ^ (at >> 1)) * size + (low ^ (k % size))


def twiddle_table(fine, per_section):
    n = np.arange(LANES) % fine
    ch = np.arange(fine)
    angle = 2.0 * math.pi * (np.outer(ch, n) % fine) / fine
    cos, sin = np.cos(angle), np.sin(angle)
    table = np.stack([np.stack([cos, -sin], 1), np.stack([sin, cos], 1)], 0)
    table = table.reshape(2, fine // per_section, per_section * 2, LANES)
    return np.ascontiguousarray(table.transpose(1, 0, 2, 3)).astype(np.float32)


def coefficients(geom, me, table_ref, coef, coef_hi, coef_lo):
    sections, rows4, u_count, chunk, n = geom
    size = n // 4
    half = chunk * rows4
    phase = lax.broadcasted_iota(jnp.int32, (1, LANES), 1) // (LANES // u_count)
    for k in range(n):
        top, kc = k // chunk * u_count * half, k % chunk
        for i in range(2):
            base = table_ref[partner(me, size, k, 1) % sections, i]
            for u in range(u_count):
                row = top + u * half + kc * rows4
                coef[row : row + rows4, i * LANES : (i + 1) * LANES] = jnp.where(phase == u, base, 0.0)
    coef_hi[...], coef_lo[...] = split(coef[...])


def filter_kernel(geom, where, x_ref, coef_hi, coef_lo, taps_ref, *outs):
    dishes, coarse, sections, rows4, u_count, j_count, spec_rows, row_count, n = geom
    me = where[0]
    size = n // 4
    chunk = n if coarse == 1 else size
    half = chunk * rows4
    fine = LANES // u_count
    phase = lax.broadcasted_iota(jnp.int32, (1, LANES), 1) // fine

    taps = [taps_ref[t : t + 1, :] for t in range(2 * u_count)]
    weights = []
    for m in range(u_count):
        inside = phase >= m
        first, second = taps[m], taps[u_count + m]
        weights.append(
            (jnp.where(inside, first, 0.0), jnp.where(inside, second, first), jnp.where(inside, 0.0, second))
        )

    def filtered(start):
        rows = [x_ref[pl.ds(start + 2 * j, spec_rows, stride=2), :] for j in range(j_count)]
        total = rows[0] * weights[0][0] + rows[1] * weights[0][1]
        for m in range(1, u_count):
            part = rows[0] * weights[m][0] + rows[1] * weights[m][1] + rows[2] * weights[m][2]
            total = total + pltpu.roll(part, LANES - m * fine, 1)
        return total

    group = u_count
    lane = lax.broadcasted_iota(jnp.int32, (8, LANES), 1)
    sub = lax.broadcasted_iota(jnp.int32, (8, LANES), 0)
    low_lane, low_sub = lane < spec_rows, sub < 4
    for kb in range(n // chunk):
        band = partner(me, size, kb * chunk, 1) // sections if coarse > 1 else 0
        mine = slice(kb * u_count * half, (kb + 1) * u_count * half)

        def step(dg, carry):
            pieces = []
            for d in range(group):
                start = ((dg * group + d) * coarse + band) * row_count * 2
                pieces.append(jnp.concatenate([filtered(start + i) for i in range(2)], axis=1))
            x = split(jnp.concatenate(pieces, axis=0))
            out = dot3((coef_hi[mine, :], coef_lo[mine, :]), x, NT)
            per_tile = 8 // rows4
            for g in range(half // 8):
                for u1 in range(2):
                    tiles = []
                    for d1 in range(2):
                        a0, a1 = (
                            out[
                                (u1 * 2 + u0) * half + g * 8 : (u1 * 2 + u0) * half + g * 8 + 8,
                                d1 * LANES : (d1 + 1) * LANES,
                            ]
                            for u0 in range(2)
                        )
                        tiles.append(jnp.where(low_lane, a0, pltpu.roll(a1, spec_rows, 1)))
                        tiles.append(jnp.where(low_lane, pltpu.roll(a0, spec_rows, 1), a1))
                    for t in range(0, group, per_tile):
                        at = pl.multiple_of((dg * group + t) * rows4, 8)
                        for kk in range(per_tile):
                            k = kb * chunk + per_tile * g + kk
                            if per_tile == 2:
                                b0, b1 = tiles[t], tiles[t + 1]
                                if kk == 0:
                                    tile = jnp.where(low_sub, b0, pltpu.roll(b1, 4, 0))
                                else:
                                    tile = jnp.where(low_sub, pltpu.roll(b0, 4, 0), b1)
                            else:
                                tile = jnp.concatenate(
                                    [b[kk * rows4 : (kk + 1) * rows4] for b in tiles[t : t + per_tile]], axis=0
                                )
                            outs[k][u1, pl.ds(at, 8), :] = tile
            return carry

        lax.fori_loop(0, dishes // group, step, 0, unroll=2)


def rows_kernel(samples, geom, x_ref, table_ref, out_ref, coef_hi, coef_lo, coef):
    full, tail = samples // LANES, samples % LANES

    def step(d, carry):
        for r in range(full):
            out_ref[d, :, r] = x_ref[0, d, :, :, r * LANES : (r + 1) * LANES]
        if tail:
            out_ref[d, :, full] = jnp.zeros(out_ref.shape[1:2] + out_ref.shape[3:], f32)
            out_ref[d, :, full, :, :tail] = x_ref[0, d, :, :, full * LANES :]
        return carry

    lax.fori_loop(0, x_ref.shape[1], step, 0)
    coefficients(geom, lax.axis_index("chan"), table_ref, coef, coef_hi, coef_lo)


def filter_bank(where, voltages, filter_taps, n):
    _, dishes, coarse, parts, samples = voltages.shape
    taps, fine = filter_taps.shape
    spectra = samples // fine - taps + 1
    per_section = coarse * fine // n
    sections = fine // per_section
    u_count = LANES // fine
    j_count = -(-(u_count - 1 + taps) * fine // LANES)
    spec_rows = spectra // u_count
    row_count = spec_rows + j_count - 1
    rows4 = per_section * 2
    assert u_count == 4 and taps == 8 and j_count == 3 and spec_rows == 64 and rows4 in (2, 4) and dishes % 4 == 0
    table = twiddle_table(fine, per_section)
    rows, width = u_count * n * rows4, 2 * LANES
    half = jax.ShapeDtypeStruct((rows, width), bf16)
    chunk = n if coarse == 1 else n // 4
    x, *coefs = pl.pallas_call(
        functools.partial(rows_kernel, samples, (sections, rows4, u_count, chunk, n)),
        in_specs=[pl.BlockSpec(memory_space=VMEM)] * 2,
        out_specs=[pl.BlockSpec(memory_space=VMEM)] * 3,
        scratch_shapes=[VMEM((rows, width), f32)],
        out_shape=[jax.ShapeDtypeStruct((dishes, coarse, row_count, parts, LANES), f32), half, half],
        compiler_params=pltpu.CompilerParams(vmem_limit_bytes=2 << 20),
        cost_estimate=pl.CostEstimate(flops=0, bytes_accessed=4 << 20, transcendentals=0),
        name="rows",
    )(voltages, jnp.asarray(table))
    x = x.reshape(dishes * coarse * row_count * parts, LANES)
    taps_rows = jnp.tile(filter_taps, (1, u_count))
    geom = (dishes, coarse, sections, rows4, u_count, j_count, spec_rows, row_count, n)
    block = jax.ShapeDtypeStruct((spectra // LANES, dishes * rows4, LANES), f32)
    return pl.pallas_call(
        functools.partial(filter_kernel, geom),
        grid_spec=pltpu.PrefetchScalarGridSpec(
            num_scalar_prefetch=1,
            grid=(1,),
            in_specs=[pl.BlockSpec(memory_space=VMEM)] * 4,
            out_specs=[pl.BlockSpec(memory_space=VMEM)] * n,
        ),
        out_shape=[block] * n,
        compiler_params=pltpu.CompilerParams(vmem_limit_bytes=12 << 20),
        cost_estimate=pl.CostEstimate(
            flops=6 * rows * width * dishes * spec_rows, bytes_accessed=5 << 20, transcendentals=0
        ),
        name="filter_bank",
    )(where, x, *coefs, taps_rows)


def gain_kernel(where, *refs):
    *pieces, hi_ref, lo_ref = refs
    beams = hi_ref.shape[1] // 2
    row = 0
    for piece in pieces:
        count = piece.shape[1]
        level = piece[0]
        quarter = PHASE_LEVELS // 4
        turn = (level + quarter // 2) // quarter
        x = (level - turn * quarter).astype(f32) * (2.0 * math.pi / PHASE_LEVELS)
        x2 = x * x
        sin = x + x * x2 * (-1.0 / 6 + x2 * (1.0 / 120 + x2 * (-1.0 / 5040 + x2 * (1.0 / 362880))))
        cos = 1.0 + x2 * (-0.5 + x2 * (1.0 / 24 + x2 * (-1.0 / 720 + x2 * (1.0 / 40320 - x2 * (1.0 / 3628800)))))
        odd = (turn & 1) == 1
        c = jnp.where(odd, sin, cos)
        s = jnp.where(odd, cos, sin)
        c = jnp.where(((turn + 1) & 2) == 2, -c, c)
        s = jnp.where((turn & 2) == 2, -s, s)
        hi_ref[0, row : row + count], lo_ref[0, row : row + count] = split(c)
        hi_ref[0, beams + row : beams + row + count], lo_ref[0, beams + row : beams + row + count] = split(s)
        row += count


def gains(where, pieces, beams, local):
    channels, _, dishes = pieces[0].shape
    out = jax.ShapeDtypeStruct((channels, 2 * beams, dishes), bf16)
    whole = pl.BlockSpec((1, 2 * beams, dishes), lambda p, w: (p, 0, 0))
    return pl.pallas_call(
        gain_kernel,
        grid_spec=pltpu.PrefetchScalarGridSpec(
            num_scalar_prefetch=1,
            grid=(channels,),
            in_specs=[
                pl.BlockSpec((1, beams if local else x.shape[1], dishes), lambda p, w: (p, w[1] if local else 0, 0))
                for x in pieces
            ],
            out_specs=[whole, whole],
        ),
        out_shape=[out, out],
        compiler_params=pltpu.CompilerParams(vmem_limit_bytes=(48 if local else 16) << 20),
        cost_estimate=pl.CostEstimate(
            flops=40 * channels * beams * dishes, bytes_accessed=12 * channels * beams * dishes, transcendentals=0
        ),
    )(where, *pieces)


def put(hi, lo, p, at, rows, col, value):
    h, l = split(value)
    hi[p, pl.ds(at, rows), col : col + value.shape[1]] = h
    lo[p, pl.ds(at, rows), col : col + value.shape[1]] = l


def unpack(blocks, first, me, base, dishes, hi, lo, full):
    channels, _, width = hi.shape
    spectra = width // 2
    count = len(blocks)
    pair = 1 if dishes % 16 == 0 else 16 // dishes
    assert pair <= 2
    rows = pair * dishes
    flip = (me % 2) == 1
    for b in range(0, count, pair):
        place = ((me ^ (first + b)) % count) // pair * rows
        for p in range(channels):
            for part in range(2):
                for u in range(spectra // LANES):
                    got = [
                        block[u, pl.ds(p * 2 + part, dishes, stride=channels * 2), :] for block in blocks[b : b + pair]
                    ]
                    if pair == 2:
                        got = [jnp.where(flip, got[1], got[0]), jnp.where(flip, got[0], got[1])]
                    value = jnp.concatenate(got, axis=0)
                    col = part * spectra + u * LANES
                    put(hi, lo, p, pl.multiple_of(base + place, rows), rows, col, value)
                    if full is not None:
                        full[p, pl.ds(pl.multiple_of(place, rows), rows), col : col + LANES] = value


def own_group_kernel(geom, group, *refs):
    _, dishes = geom
    size = LANES // dishes
    blocks = refs[:size]
    outs = refs[size:] if group % 2 == 0 else refs[size + 2 :]
    hi, lo = outs[:2]
    full = outs[2] if len(outs) > 2 else None
    me = lax.axis_index("chan")
    base = group % 2 * LANES
    unpack(blocks, group * size, me, base, dishes, hi, lo, full)


def own_group(geom, group, blocks, pair, channels, spectra, send):
    half = jax.ShapeDtypeStruct((channels, 2 * LANES, 2 * spectra), bf16)
    full = jax.ShapeDtypeStruct((channels, LANES, 2 * spectra), f32)
    whole = pl.BlockSpec(memory_space=VMEM)
    out = [half, half] + ([full] if send else [])
    at = len(blocks)
    return pl.pallas_call(
        functools.partial(own_group_kernel, geom, group),
        in_specs=[whole] * (len(blocks) + len(pair)),
        out_specs=[whole] * len(out),
        out_shape=out,
        input_output_aliases={at: 0, at + 1: 1} if pair else {},
        compiler_params=pltpu.CompilerParams(vmem_limit_bytes=2 << 20),
        cost_estimate=pl.CostEstimate(flops=1 << 20, bytes_accessed=2 << 20, transcendentals=0),
    )(*blocks, *pair)


def turned(x):
    half = x.shape[1] // 2
    return jnp.concatenate([-x[:, half:], x[:, :half]], axis=1)


def beam_terms(g_hi, g_lo, p, ats, x):
    hi, lo = ([g[p, :, pl.ds(pl.multiple_of(at, LANES), LANES)] for at in ats] for g in (g_hi, g_lo))
    left = jnp.concatenate(hi + hi + lo, axis=1)
    right = jnp.concatenate([x[0], x[1], x[0]], axis=0)
    return lax.dot_general(left, right, NN, preferred_element_type=f32)


class Writer:
    def __init__(self, vis, stage, sems, scale):
        self.vis, self.stage, self.sems, self.scale = vis, stage, sems, scale
        self.slots, self.copies = 0, []

    def put(self, p, v, rows, cols, value):
        slot = self.slots
        self.slots += 1
        self.stage[slot] = value * self.scale
        for i, row in enumerate(rows):
            for j, col in enumerate(cols):
                source = self.stage.at[slot, i * LANES : (i + 1) * LANES, j * LANES : (j + 1) * LANES]
                target = self.vis.at[
                    p, v, pl.ds(pl.multiple_of(row, LANES), LANES), pl.ds(pl.multiple_of(col, LANES), LANES)
                ]
                copy = pltpu.make_async_copy(source, target, self.sems.at[len(self.copies)])
                copy.start()
                self.copies.append(copy)

    def wide(self, p, rows, cols, left, right):
        self.put(p, 0, rows, cols, dot3(left, right, NT))
        self.put(p, 1, rows, cols, dot3(left, tuple(turned(r) for r in right), NT))

    def narrow(self, p, rows, cols, left, right):
        both = dot3(left, tuple(jnp.concatenate([r, turned(r)], axis=0) for r in right), NT)
        width = right[0].shape[0]
        self.put(p, 0, rows, cols, both[:, :width])
        self.put(p, 1, rows, cols, both[:, width:])

    def finish(self):
        for copy in self.copies:
            copy.wait()


def places(geom):
    n, dishes = geom
    size = LANES // dishes
    me, quad = lax.axis_index("chan"), lax.axis_index("quad")
    at = [partner(me, size, g * size, -1) // size * LANES for g in range(4)]
    total = n * dishes
    return at, quad * total, (1 - quad) * total


def first_kernel(geom, *refs):
    own_hi, own_lo, far0, far1, gho, glo, ghf, glf, vis, q_ref, far_hi, far_lo, stage, sems = refs
    channels, _, width = own_hi.shape
    at, here, there = places(geom)
    near = at[:2]
    out = Writer(vis, stage, sems, 2.0 / width)
    for p in range(channels):
        for g, far in enumerate((far0, far1)):
            put(far_hi, far_lo, p, g * LANES, LANES, 0, far[p])
        mine, theirs = (own_hi[p], own_lo[p]), (far_hi[p], far_lo[p])
        out.wide(p, near, [here + a for a in near], mine, mine)
        out.wide(p, near, [there + a for a in near], mine, theirs)
        q_ref[p] = beam_terms(gho, glo, p, near, mine) + beam_terms(ghf, glf, p, near, theirs)
    out.finish()


def second_kernel(geom, *refs):
    near_hi, near_lo, own_hi, own_lo, far_hi, far_lo, gho, glo, q_in, _, vis, q_ref, stage, sems = refs
    channels, _, width = own_hi.shape
    at, here, there = places(geom)
    near, away = at[:2], at[2:]
    out = Writer(vis, stage, sems, 2.0 / width)
    for p in range(channels):
        first, mine, theirs = (near_hi[p], near_lo[p]), (own_hi[p], own_lo[p]), (far_hi[p], far_lo[p])
        out.wide(p, away, [here + a for a in away], mine, mine)
        out.wide(p, away, [here + a for a in near], mine, first)
        out.wide(p, near, [here + a for a in away], first, mine)
        out.wide(p, away, [there + a for a in near], mine, theirs)
        q_ref[p] = q_in[p] + beam_terms(gho, glo, p, away, mine)
    out.finish()


def late_kernel(geom, group, raw, *refs):
    n, dishes = geom
    size = LANES // dishes
    got, refs = refs[: size if raw else 1], refs[size if raw else 1 :]
    near_hi, near_lo, own_hi, own_lo, ghf, glf, q_in, _, vis, q_ref, stage, sems = refs[:12]
    hi, lo, *more = refs[12:]
    channels, _, width = own_hi.shape
    at, _, there = places(geom)
    col = there + at[group]
    if raw:
        unpack(got, group * size, lax.axis_index("chan"), 0, dishes, hi, lo, None)
    out = Writer(vis, stage, sems, 2.0 / width)
    copies = []
    for p in range(channels):
        if not raw:
            put(hi, lo, p, 0, LANES, 0, got[0][p])
        q = q_in[p] + beam_terms(ghf, glf, p, [at[group]], (hi[p], lo[p]))
        if not raw:
            q_ref[p] = q
            continue
        held, held_sems = more
        beams, spectra = q.shape[0] // 2, q.shape[1] // 2
        re = q[:beams, :spectra] + q[beams:, spectra:]
        im = q[:beams, spectra:] - q[beams:, :spectra]
        power = (re * re + im * im) * (1.0 / (2 * n * dishes))
        lane = lax.broadcasted_iota(jnp.int32, (beams, LANES), 1)
        for h in range(spectra // LANES):
            at_lane = lane % 2 * 64 + 32 * h + lane // 4
            low, high = (
                jnp.take_along_axis(power[:, i * LANES : (i + 1) * LANES], at_lane, axis=1, mode="promise_in_bounds")
                for i in range(2)
            )
            held[p, :, h * LANES : (h + 1) * LANES] = jnp.where(lane % 4 < 2, low, high)
        copy = pltpu.make_async_copy(held.at[p], q_ref.at[p], held_sems.at[p])
        copy.start()
        copies.append(copy)
    for p in range(channels):
        x = (hi[p], lo[p])
        out.narrow(p, at[:2], [col], (near_hi[p], near_lo[p]), x)
        out.narrow(p, at[2:], [col], (own_hi[p], own_lo[p]), x)
    for copy in copies:
        copy.wait()
    out.finish()


def products(kernel, ins, outs, aliases, slots, block, more, flops, last=False):
    whole, where_it_is = pl.BlockSpec(memory_space=VMEM), pl.BlockSpec(memory_space=pl.ANY)
    vis_shape = outs[0].shape
    return pl.pallas_call(
        kernel,
        in_specs=[where_it_is if x.shape == vis_shape else whole for x in ins],
        out_specs=[where_it_is] + [where_it_is if x.dtype == f32 and last else whole for x in outs[1:]],
        scratch_shapes=[VMEM((slots,) + block, f32), pltpu.SemaphoreType.DMA((4 * slots,))] + more,
        out_shape=outs,
        input_output_aliases=aliases,
        compiler_params=pltpu.CompilerParams(vmem_limit_bytes=16 << 20),
        cost_estimate=pl.CostEstimate(flops=flops, bytes_accessed=4 << 20, transcendentals=0),
    )(*ins)


def phase_kernel(beams, first, phases, out, sems):
    channels, count, _ = out.shape
    pieces = sems.shape[0] // channels
    rows = count // pieces
    at = (1 - lax.axis_index("quad")) * beams + first
    copies = []
    for p in range(channels):
        for i in range(pieces):
            copies.append(
                pltpu.make_async_copy(
                    phases.at[p, pl.ds(pl.multiple_of(at + i * rows, rows), rows), :],
                    out.at[p, i * rows : (i + 1) * rows, :],
                    sems.at[p * pieces + i],
                )
            )
    for copy in copies:
        copy.start()
    for copy in copies:
        copy.wait()


def phase_piece(phases, beams, first, count):
    channels, _, dishes = phases.shape
    pieces = count // 32
    return pl.pallas_call(
        functools.partial(phase_kernel, beams, first),
        in_specs=[pl.BlockSpec(memory_space=pltpu.HBM)],
        out_specs=pl.BlockSpec(memory_space=VMEM),
        scratch_shapes=[pltpu.SemaphoreType.DMA((pieces * channels,))],
        out_shape=jax.ShapeDtypeStruct((channels, count, dishes), jnp.int32),
        compiler_params=pltpu.CompilerParams(vmem_limit_bytes=52 << 20),
        cost_estimate=pl.CostEstimate(flops=0, bytes_accessed=2 << 20, transcendentals=0),
    )(phases)


def per_device(n, n_quad, voltages, filter_taps, phases):
    return whole_step(n, n_quad, voltages, filter_taps, phases)


def whole_step(n, n_quad, voltages, filter_taps, phases):
    dishes = voltages.shape[1]
    channels, beams_all, _ = phases.shape
    beams = beams_all // n_quad
    size = LANES // dishes
    groups = n // size
    assert groups == 4
    geom = (n, dishes)
    me = lax.axis_index("chan").astype(jnp.int32)
    quad = lax.axis_index("quad").astype(jnp.int32)
    where = jnp.stack([me, quad])
    swap = [(0, 1), (1, 0)]

    received = []
    for first, count in ((0, beams),):
        piece = phase_piece(phases, beams, first, count)
        received.append(lax.ppermute(piece, "quad", swap))

    sent = filter_bank(where, voltages, filter_taps, n)
    spectra = sent[0].shape[0] * LANES

    own = []
    for k in range(n):
        route = [(i, partner(i, size, k, 1)) for i in range(n)]
        own.append(lax.ppermute(sent[k], "chan", route) if k else sent[k])

    pairs = {0: [], 1: []}
    far = []
    for g in range(groups):
        last = g == groups - 1
        blocks = own[g * size : (g + 1) * size]
        got = own_group(geom, g, blocks, pairs[g // 2], channels, spectra, not last)
        pairs[g // 2] = got[:2]
        if not last:
            far.append(lax.ppermute(got[2], "quad", swap))
    raw = []
    for k in range((groups - 1) * size, n):
        raw.append(lax.ppermute(own[k], "quad", swap))

    own_gains = gains(where, [phases], beams, True)
    far_gains = gains(where, received, beams, False)

    total = n * dishes
    vis_shape = jax.ShapeDtypeStruct((channels, 2, total, n_quad * total), f32)
    q_shape = jax.ShapeDtypeStruct((channels, 2 * beams, 2 * spectra), f32)
    p_shape = jax.ShapeDtypeStruct((channels, beams, spectra), f32)
    half = jax.ShapeDtypeStruct((channels, 2 * LANES, 2 * spectra), bf16)
    near, away = pairs[0], pairs[1]
    wide, narrow = (2 * LANES, 2 * LANES), (2 * LANES, LANES)
    unit = channels * 6 * 2 * (2 * LANES) * (2 * LANES) * 2 * spectra
    late = [VMEM((channels, LANES, 2 * spectra), bf16)] * 2
    power = [VMEM((channels, beams, spectra), f32), pltpu.SemaphoreType.DMA((channels,))]

    vis, q, far_hi, far_lo = products(
        functools.partial(first_kernel, geom),
        [*near, far[0], far[1], *own_gains, *far_gains],
        [vis_shape, q_shape, half, half], {}, 4 * channels, wide, [], 4 * unit,
    )
    vis, q = products(
        functools.partial(second_kernel, geom),
        [*near, *away, far_hi, far_lo, *own_gains, q, vis],
        [vis_shape, q_shape], {8: 1, 9: 0}, 8 * channels, wide, [], 5 * unit,
    )
    vis, q = products(
        functools.partial(late_kernel, geom, 2, False),
        [far[2], *near, *away, *far_gains, q, vis],
        [vis_shape, q_shape], {7: 1, 8: 0}, 4 * channels, narrow, late, 2 * unit,
    )
    vis, power = products(
        functools.partial(late_kernel, geom, 3, True),
        [*raw, *near, *away, *far_gains, q, vis],
        [vis_shape, p_shape], {size + 7: 0}, 4 * channels, narrow, late + power, 2 * unit, True,
    )
    return vis, power


def solution(mesh):
    n, n_quad = mesh.shape["chan"], mesh.shape["quad"]
    assert n_quad == 2 and n & (n - 1) == 0
    return jax.shard_map(
        functools.partial(per_device, n, n_quad),
        mesh=mesh,
        in_specs=(P("quad", "chan", None, None, None), P(), P("chan", None, "quad")),
        out_specs=(P("chan", None, "quad", None), P("chan", "quad", None)),
        check_vma=False,
    )
```
